256 devices in a mesh: row: 4 (over x), col: 64 (over y, z, core).
Axes of the slice: x: 4, y: 4, z: 8, core: 2. Of those that a mesh axis runs over, the one named last changes fastest.
Arguments:
- activations: bfloat16 [8, 256, 8192], P('row')
- out_grads: bfloat16 [8, 256, 28672], P('row', None, 'col')
- valid_len: int32 [8], P('row'), may hold values from 1 to 256, 1024 in all
- weight: bfloat16 [8192, 28672], P('row', 'col'), may hold values from -0.0625 to 0.0625
- sketch: bfloat16 [28672, 512], P('col'), may hold values from -6 to 6
Outputs:
- basis: float32 [8192, 512], P(('row', 'col'))
- coeffs: float32 [512, 28672], P('row', 'col')
The draws below stay inside these ranges and needn't reach their ends.
Inputs may be any that keep to these rules, and one draw needn't show every extreme that they name: `valid_len`: valid tokens of each sequence; at least one sequence fills all 256 slots.
All inputs are finite; a program needn't handle non-finite values. No bound on the sum of `valid_len` on one device may be relied on, other than what follows from the above.
Results may differ from the reference program's by a relative error of at most 0.01.
Values may be sent and summed in bfloat16 or wider, within the bound.
A program may use at most 64 MiB of HBM per device.

```python
import math
import jax
import jax.numpy as jnp
import numpy as np
from jax import lax

D = 8192
FF = 28672
RANK = 512
LEN = 256
SEQS = 8
N_COL = 64


def draw_activations(key, part):
    key_scale = jax.random.fold_in(key, 0)
    key_base = jax.random.fold_in(key, 1)
    key_mix = jax.random.fold_in(key, 3)
    feature_scale = jnp.exp(jax.random.uniform(key_scale, (D,), jnp.float32, jnp.log(0.3), jnp.log(3.0)))
    feature_scale = feature_scale * (1.0 + 0.8 * jnp.arange(D, dtype=jnp.float32) / D)
    seq_feature = jnp.exp(jax.random.uniform(key_mix, (SEQS, 1, D), jnp.float32, jnp.log(0.1), jnp.log(10.0)))
    base = jax.random.normal(key_base, (SEQS, LEN, D), jnp.float32)
    return (base * seq_feature * feature_scale).astype(jnp.bfloat16)


def draw_out_grads(key, part):
    key_scale, key_base = jax.random.split(key, 2)
    column_scale = jnp.exp(jax.random.uniform(key_scale, (FF,), jnp.float32, jnp.log(0.5), jnp.log(2.0)))
    column_scale = column_scale * (0.6 + 1.2 * jnp.arange(FF, dtype=jnp.float32) / FF)
    base = jnp.clip(jax.random.normal(key_base, (SEQS, LEN, FF), jnp.float32), -4.0, 4.0)
    return (base * column_scale).astype(jnp.bfloat16)


def level_of(stream_key, extent, cuts, low, largest):
    loudness, own = 1.0, jax.random.fold_in(stream_key, 6)
    for position, blocks in cuts:
        steps = jnp.exp(jax.random.uniform(jax.random.fold_in(own, position), (blocks,), jnp.float32, low / len(cuts), largest / len(cuts)))
        loudness = loudness * jnp.repeat(steps, extent[position] // blocks).reshape([-1 if axis == position else 1 for axis in range(len(extent))])
    return loudness


def length_profile(number_of, total, reach, lean):
    weights = [(1 << 20) // math.isqrt(grade ** lean) + 1 for grade in range(2, number_of + 1)]
    surplus, counts = total - reach - (number_of - 1), [1] * (number_of - 1)
    while surplus > 0:
        free = [i for i in range(number_of - 1) if counts[i] < reach]
        pool, left = sum([weights[i] for i in free]), surplus
        for i in free:
            addition = min(reach - counts[i], max(1, left * weights[i] // pool), surplus)
            counts[i] = counts[i] + addition
            surplus = surplus - addition
    return np.array([reach] + counts)


def uneven(own_key, amount, total, limit, lean):
    if amount == 2:
        one = jax.random.randint(own_key, (), max(1, total - limit), min(limit, total - 1) + 1)
        return jnp.stack([one, total - one])
    tallies = jnp.asarray(length_profile(amount, total, limit, lean), jnp.int32)
    twos = (amount - 1) // 2
    giver, taker = tallies[1:1 + 2 * twos:2], tallies[2:2 + 2 * twos:2]
    room = jnp.minimum(giver - 1, limit - taker)
    shifted = jax.random.randint(jax.random.fold_in(own_key, 1), (twos,), 0, 1 << 20) % (room + 1)
    tallies = tallies.at[1:1 + 2 * twos:2].set(giver - shifted).at[2:2 + 2 * twos:2].set(taker + shifted)
    return tallies[jax.random.permutation(jax.random.fold_in(own_key, 2), amount)]


def bell_draw(rng, dims, spread, reach, pieces=(), held_as=jnp.bfloat16):
    result = spread * jax.random.normal(rng, dims, jnp.float32)
    if pieces:
        result = result * level_of(rng, dims, pieces, -0.22, 0.18)
    return jnp.clip(result, -reach, reach).astype(held_as)


def setup_inputs(seed: int = 0) -> dict:
    splits = jax.random.split(jax.random.key(seed), 6)
    activations = draw_activations(jax.random.fold_in(splits[5], 71), 0)
    out_grads = draw_out_grads(jax.random.fold_in(splits[5], 71), 0)
    valid_len = uneven(splits[2], SEQS, SEQS * LEN // 2, LEN, 0).astype(jnp.int32)
    weight = bell_draw(splits[3], (D, FF), D ** -0.5, 0.0625, ((0, 4), (1, 64)))
    sketch = bell_draw(splits[4], (FF, RANK), 1.0, 6.0, ((0, 64),))
    return dict(activations=activations, out_grads=out_grads, valid_len=valid_len, weight=weight, sketch=sketch)


def contract_rows(left, right):
    return lax.dot_general(left.astype(jnp.float32), right.astype(jnp.float32), (((0,), (0,)), ((), ())), preferred_element_type=jnp.float32)

def orthonormal(sketch_rows):
    gram = lax.dot_general(sketch_rows, sketch_rows, (((0,), (0,)), ((), ())), precision=lax.Precision.HIGHEST)
    factor_low = jnp.linalg.cholesky(gram)
    return lax.linalg.triangular_solve(factor_low, sketch_rows, left_side=False, lower=True, transpose_a=True)

def reference(activations, out_grads, valid_len, weight, sketch):
    block_cols = FF // N_COL
    positions = jnp.arange(LEN, dtype=jnp.int32)

    def seq_mass(seq_index):
        valid = (positions < valid_len[seq_index]).astype(jnp.bfloat16)
        inputs = activations[seq_index]
        masked = out_grads[seq_index] * valid[:, None]

        def add_block(running, block_index):
            columns = lax.dynamic_slice_in_dim(masked, (block_index * block_cols).astype(jnp.int32), block_cols, 1)
            grad_block = contract_rows(inputs, columns)
            return (running + lax.optimization_barrier(jnp.sum(grad_block * grad_block, axis=1)), None)
        mass, unused = lax.scan(add_block, jnp.zeros((D,), jnp.float32), jnp.arange(N_COL, dtype=jnp.int32))
        return mass
    fisher = lax.optimization_barrier(jnp.sum(lax.map(seq_mass, jnp.arange(SEQS, dtype=jnp.int32)), axis=0))
    total_mass = jnp.sum(fisher)
    row_scale = jnp.sqrt(fisher / (total_mass / D + 1e-06))
    first_sketch = (row_scale[:, None] * jnp.dot(weight.astype(jnp.float32), sketch.astype(jnp.float32), preferred_element_type=jnp.float32)).astype(jnp.bfloat16)
    scaled = (row_scale[:, None] * weight.astype(jnp.float32)).astype(jnp.bfloat16)
    projected = contract_rows(scaled, first_sketch).astype(jnp.bfloat16)
    second_sketch = jnp.dot(scaled.astype(jnp.float32), projected.astype(jnp.float32), preferred_element_type=jnp.float32)
    second_basis = orthonormal(second_sketch)
    coeff_raw = contract_rows(second_basis.astype(jnp.bfloat16), scaled)
    return (second_basis * D ** 0.5, coeff_raw * FF ** 0.5)
```

```python
import functools
import math

import jax
import jax.numpy as jnp
from jax import lax
from jax.experimental import pallas as pl
from jax.experimental.pallas import tpu as pltpu
from jax.sharding import PartitionSpec as P

MESH = pl.DeviceIdType.MESH
VMEM = pl.BlockSpec(memory_space=pltpu.VMEM)
F32, BF16 = jnp.float32, jnp.bfloat16
ROWS, COLS, RANK, DIM, FF = 2048, 448, 512, 8192, 28672
HALF, YCH, ZCH = 1024, 256, 32
PIECES = 4
WIDE = RANK // PIECES
ZTYPE = F32


def f32(ref):
    return ref[...].astype(F32)


def at_rows(ref, start, count, step=16):
    return ref.at[pl.ds(pl.multiple_of(start, step), count)]


class Net:
    def __init__(self, send_sems, recv_sems):
        self.send_sems, self.recv_sems, self.copies = send_sems, recv_sems, []

    def send(self, src, dst, device):
        slot = len(self.copies)
        copy = pltpu.make_async_remote_copy(
            src_ref=src,
            dst_ref=dst,
            send_sem=self.send_sems.at[slot],
            recv_sem=self.recv_sems.at[slot],
            device_id=device,
            device_id_type=MESH,
        )
        copy.start()
        self.copies.append(copy)
        return copy

    def drain(self):
        for copy in self.copies:
            copy.wait_send()


def greet(peers):
    barrier = pltpu.get_barrier_semaphore()
    for peer in peers:
        pl.semaphore_signal(barrier, inc=1, device_id=peer, device_id_type=MESH)
    pl.semaphore_wait(barrier, len(peers))


def place():
    row, col = lax.axis_index("row"), lax.axis_index("col")
    return row, col, lax.rem(col, 2), lax.rem(col // 2, 8), col // 16


class Ring:
    def __init__(self, net, me, up, down, chunk, front):
        self.net, self.up, self.down, self.front, self.back = net, up, down, front, chunk - front
        self.own = me * chunk
        self.next = lax.rem(me + 1, 4) * chunk
        self.far = lax.rem(me + 2, 4) * chunk
        self.last = lax.rem(me + 3, 4) * chunk

    def reduce_start(self, src, got_f, got_b):
        send, front, back = self.net.send, self.front, self.back
        self.red = [
            send(src(self.far, front), got_f.at[0], self.up),
            send(src(self.far + front, back), got_b.at[0], self.down),
            send(src(self.next + front, back), got_b.at[1], self.up),
            send(src(self.last, front), got_f.at[1], self.down),
        ]

    def reduce_relay(self, src, got_f, got_b, sum_f, sum_b):
        send, front, back = self.net.send, self.front, self.back
        self.red[0].wait_recv()
        sum_f[...] = (f32(got_f.at[0]) + f32(src(self.next, front))).astype(sum_f.dtype)
        self.red.append(send(sum_f, got_f.at[2], self.up))
        self.red[1].wait_recv()
        sum_b[...] = (f32(got_b.at[0]) + f32(src(self.last + front, back))).astype(sum_b.dtype)
        self.red.append(send(sum_b, got_b.at[2], self.down))

    def reduce_end(self, src, got_f, got_b):
        for copy in self.red[2:]:
            copy.wait_recv()
        top = f32(src(self.own, self.front)) + f32(got_f.at[1]) + f32(got_f.at[2])
        low = f32(src(self.own + self.front, self.back)) + f32(got_b.at[1]) + f32(got_b.at[2])
        return top, low

    def gather_start(self, dst):
        whole = dst(self.own, self.front + self.back)
        self.gat = [self.net.send(whole, whole, self.up), self.net.send(whole, whole, self.down)]

    def gather_relay(self, dst):
        self.gat[0].wait_recv()
        part = dst(self.last, self.front)
        self.gat.append(self.net.send(part, part, self.up))
        self.gat[1].wait_recv()
        part = dst(self.next + self.front, self.back)
        self.gat.append(self.net.send(part, part, self.down))

    def gather_end(self):
        self.gat[2].wait_recv()
        self.gat[3].wait_recv()


def col_sum_steps(net, x_ref, o_ref, scale_ref, square, pair, mine, got_f, got_b, sum_f, sum_b, ysum, zgot):
    row, _, core, z, y = place()

    def at(yy, zz, kk):
        return (row, (yy * 8 + zz) * 2 + kk)

    partner = at(y, z, 1 - core)
    up, down = at(lax.rem(y + 1, 4), z, core), at(lax.rem(y + 3, 4), z, core)
    zpeer = [at(y, lax.rem(z + d, 8), core) for d in range(1, 8)]
    base, other = core * HALF, (1 - core) * HALF
    state = [dict() for _ in range(PIECES)]

    def cols(p):
        return pl.ds(p * WIDE, WIDE)

    def out(p, start, count):
        return o_ref.at[pl.ds(pl.multiple_of(base + start, 16), count), cols(p)]

    def src(p):
        return lambda start, count: mine.at[p, pl.ds(pl.multiple_of(start, 16), count)]

    def own_scale():
        start = base + y * YCH + z * ZCH
        line = scale_ref[pl.ds(start // 128, 1), :]
        lanes = lax.broadcasted_iota(jnp.int32, (ZCH, 128), 1)
        rows = lax.broadcasted_iota(jnp.int32, (ZCH, 128), 0)
        picked = jnp.where(lanes == rows + lax.rem(start, 128), line, 0.0)
        scale = jnp.sum(picked, axis=1, keepdims=True)
        return scale * scale if square else scale

    def s0(p):
        half = x_ref.at[pl.ds(pl.multiple_of(other, 16), HALF), cols(p)]
        state[p]["pair"] = net.send(half, pair.at[p], partner)

    def s1(p):
        state[p]["pair"].wait_recv()
        own = x_ref.at[pl.ds(pl.multiple_of(base, 16), HALF), cols(p)]
        mine[p] = (f32(own) + f32(pair.at[p])).astype(BF16)
        ring = Ring(net, y, up, down, YCH, YCH // 2)
        state[p]["ring"] = ring
        ring.reduce_start(src(p), got_f.at[p], got_b.at[p])

    def s2(p):
        state[p]["ring"].reduce_relay(src(p), got_f.at[p], got_b.at[p], sum_f.at[p], sum_b.at[p])

    def s3(p):
        top, low = state[p]["ring"].reduce_end(src(p), got_f.at[p], got_b.at[p])
        ysum[p, pl.ds(0, YCH // 2)] = top.astype(ZTYPE)
        ysum[p, pl.ds(YCH // 2, YCH // 2)] = low.astype(ZTYPE)
        state[p]["z"] = []
        for d in range(1, 8):
            part = ysum.at[p, pl.ds(pl.multiple_of(lax.rem(z + d, 8) * ZCH, 16), ZCH)]
            state[p]["z"].append(net.send(part, zgot.at[p, d - 1], zpeer[d - 1]))

    def s4(p):
        total = f32(ysum.at[p, pl.ds(pl.multiple_of(z * ZCH, 16), ZCH)])
        for d in range(7):
            state[p]["z"][d].wait_recv()
            total = total + f32(zgot.at[p, d])
        part = out(p, y * YCH + z * ZCH, ZCH)
        part[...] = (total * own_scale()).astype(BF16)
        state[p]["g"] = [net.send(part, part, peer) for peer in zpeer]

    def s5(p):
        for copy in state[p]["g"]:
            copy.wait_recv()
        ring = state[p]["ring"]
        ring.gather_start(functools.partial(out, p))
        whole = out(p, ring.own, YCH)
        state[p]["c"] = [net.send(whole, whole, partner)]

    def s6(p):
        ring = state[p]["ring"]
        ring.gather_relay(functools.partial(out, p))
        for start in (ring.last, ring.next):
            whole = out(p, start, YCH)
            state[p]["c"].append(net.send(whole, whole, partner))

    def s7(p):
        ring = state[p]["ring"]
        ring.gather_end()
        whole = out(p, ring.far, YCH)
        state[p]["c"].append(net.send(whole, whole, partner))

    def s8(p):
        for copy in state[p]["c"]:
            copy.wait_recv()

    return [s0, s1, s2, s3, s4, s5, s6, s7, s8], [partner, up, down] + zpeer


COL_COPIES = PIECES * 29
COL_SCRATCH = [
    pltpu.VMEM((PIECES, HALF, WIDE), F32),
    pltpu.VMEM((PIECES, HALF, WIDE), BF16),
    pltpu.VMEM((PIECES, 3, YCH // 2, WIDE), BF16),
    pltpu.VMEM((PIECES, 3, YCH // 2, WIDE), BF16),
    pltpu.VMEM((PIECES, YCH // 2, WIDE), BF16),
    pltpu.VMEM((PIECES, YCH // 2, WIDE), BF16),
    pltpu.VMEM((PIECES, YCH, WIDE), ZTYPE),
    pltpu.VMEM((PIECES, 7, ZCH, WIDE), ZTYPE),
]


ORDER = (0.0, 2.5, 5.0, 7.5, 14.0, 19.0, 22.0, 24.5, 26.0)
GAPS = (0.1, 1.8, 2.2, 2.2, 4.0, 4.0, 4.0, 4.0, 4.0)


def run_steps(steps, extra=()):
    events = [(ORDER[s] + GAPS[s] * p, s, p) for s in range(len(steps)) for p in range(PIECES)]
    events += [(when, -1, n) for n, (when, _) in enumerate(extra)]
    for _, s, n in sorted(events):
        if s < 0:
            extra[n][1]()
        else:
            steps[s](n)


def col_sum_kernel(x_ref, scale_ref, o_ref, send_sems, recv_sems, *scratch):
    net = Net(send_sems, recv_sems)
    steps, peers = col_sum_steps(net, x_ref, o_ref, scale_ref, False, *scratch)
    greet(peers)
    run_steps(steps)
    net.drain()


def first_kernel(x_ref, f_ref, o_ref, scale_ref, send_sems, recv_sems, fx, f1, fc, f2, fy, f3, fz, ft, fg, *scratch):
    net = Net(send_sems, recv_sems)
    steps, peers = col_sum_steps(net, x_ref, o_ref, scale_ref, True, *scratch)
    row, col, core, z, y = place()
    xpeer = [(lax.rem(row + d, 4), col) for d in range(1, 4)]
    far = (row, (lax.rem(y + 2, 4) * 8 + z) * 2 + core)
    ypeer = [peers[1], far, peers[2]]
    state = {}

    def t0():
        state["x"] = [
            net.send(at_rows(f_ref, lax.rem(row + d, 4) * 16, 16, 8), fx.at[d - 1], xpeer[d - 1])
            for d in range(1, 4)
        ]

    def t1():
        for copy in state["x"]:
            copy.wait_recv()
        f1[...] = at_rows(f_ref, row * 16, 16, 8)[...] + fx[0] + fx[1] + fx[2]
        state["c"] = net.send(f1, fc, peers[0])

    def t2():
        state["c"].wait_recv()
        f2[...] = f1[...] + fc[...]
        state["y"] = [net.send(f2, fy.at[d], ypeer[d]) for d in range(3)]

    def t3():
        for copy in state["y"]:
            copy.wait_recv()
        f3[...] = f2[...] + fy[0] + fy[1] + fy[2]
        state["z"] = [net.send(f3, fz.at[d], peers[3 + d]) for d in range(7)]

    def t4():
        total = f3[...]
        for d in range(7):
            state["z"][d].wait_recv()
            total = total + fz[d]
        scale_ref[...] = total
        ft[...] = total[0:8] + total[8:16]
        state["t"] = [net.send(ft, fg.at[d], xpeer[d]) for d in range(3)]

    def t5():
        for copy in state["t"]:
            copy.wait_recv()
        mass = jnp.sum(ft[...] + fg[0] + fg[1] + fg[2], keepdims=True)
        scale_ref[...] = jnp.sqrt(scale_ref[...] / (mass / DIM + 1e-06))

    greet(peers + [far] + xpeer)
    run_steps(steps, ((-1.0, t0), (2.6, t1), (3.9, t2), (7.0, t3), (11.5, t4), (13.9, t5)))
    net.drain()


def params(collective_id, mib):
    return pltpu.CompilerParams(
        collective_id=collective_id, has_side_effects=True, vmem_limit_bytes=mib << 20
    )


def first_sums(raw, mass):
    piece = (16, 128)
    return pl.pallas_call(
        first_kernel,
        out_shape=(jax.ShapeDtypeStruct((ROWS, RANK), BF16), jax.ShapeDtypeStruct(piece, F32)),
        in_specs=[VMEM, VMEM],
        out_specs=(VMEM, VMEM),
        scratch_shapes=[
            pltpu.SemaphoreType.DMA((COL_COPIES + 17,)),
            pltpu.SemaphoreType.DMA((COL_COPIES + 17,)),
            pltpu.VMEM((3,) + piece, F32),
            pltpu.VMEM(piece, F32),
            pltpu.VMEM(piece, F32),
            pltpu.VMEM(piece, F32),
            pltpu.VMEM((3,) + piece, F32),
            pltpu.VMEM(piece, F32),
            pltpu.VMEM((7,) + piece, F32),
            pltpu.VMEM((8, 128), F32),
            pltpu.VMEM((3, 8, 128), F32),
        ]
        + COL_SCRATCH,
        compiler_params=params(0, 28),
        name="first_sums",
    )(raw, mass)


def col_sum(x, scale):
    return pl.pallas_call(
        col_sum_kernel,
        out_shape=jax.ShapeDtypeStruct((ROWS, RANK), BF16),
        in_specs=[VMEM, VMEM],
        out_specs=VMEM,
        scratch_shapes=[
            pltpu.SemaphoreType.DMA((COL_COPIES,)),
            pltpu.SemaphoreType.DMA((COL_COPIES,)),
        ]
        + COL_SCRATCH,
        compiler_params=params(1, 28),
        name="col_sum",
    )(x, scale)


def ring_scratch(copies, front, back, width, dtype):
    return [
        pltpu.SemaphoreType.DMA((copies,)),
        pltpu.SemaphoreType.DMA((copies,)),
        pltpu.VMEM((3, front, width), dtype),
        pltpu.VMEM((3, back, width), dtype),
        pltpu.VMEM((front, width), dtype),
        pltpu.VMEM((back, width), dtype),
    ]


def row_ring(net, chunk, front):
    row, col, _, _, _ = place()
    up, down = (lax.rem(row + 1, 4), col), (lax.rem(row + 3, 4), col)
    return Ring(net, row, up, down, chunk, front), [up, down]


def row_sum_kernel(x_ref, o_ref, send_sems, recv_sems, got_f, got_b, sum_f, sum_b):
    net = Net(send_sems, recv_sems)
    ring, peers = row_ring(net, 112, 64)
    greet(peers)
    src, dst = functools.partial(at_rows, x_ref), functools.partial(at_rows, o_ref)
    ring.reduce_start(src, got_f, got_b)
    ring.reduce_relay(src, got_f, got_b, sum_f, sum_b)
    top, low = ring.reduce_end(src, got_f, got_b)
    dst(ring.own, 64)[...] = top.astype(BF16)
    dst(ring.own + 64, 48)[...] = low.astype(BF16)
    ring.gather_start(dst)
    ring.gather_relay(dst)
    ring.gather_end()
    net.drain()


def row_sum(x):
    return pl.pallas_call(
        row_sum_kernel,
        out_shape=jax.ShapeDtypeStruct((COLS, RANK), BF16),
        in_specs=[VMEM],
        out_specs=VMEM,
        scratch_shapes=ring_scratch(10, 64, 48, RANK, BF16),
        compiler_params=params(2, 8),
        name="row_sum",
    )(x)


def gram_kernel(y_ref, o_ref, send_sems, recv_sems, got_f, got_b, sum_f, sum_b, own):
    net = Net(send_sems, recv_sems)
    row, col, core, z, y = place()
    partner = (row, (y * 8 + z) * 2 + 1 - core)
    ring, peers = row_ring(net, 64, 32)
    half = core * 256
    left = y_ref[:, pl.ds(pl.multiple_of(half, 128), 256)]
    own[...] = lax.dot_general(left, y_ref[...], (((0,), (0,)), ((), ())), preferred_element_type=F32)
    greet(peers + [partner])
    src = functools.partial(at_rows, own, step=8)

    def dst(start, count):
        return at_rows(o_ref, half + start, count, 8)

    ring.reduce_start(src, got_f, got_b)
    ring.reduce_relay(src, got_f, got_b, sum_f, sum_b)
    top, low = ring.reduce_end(src, got_f, got_b)
    dst(ring.own, 32)[...] = top
    dst(ring.own + 32, 32)[...] = low
    ring.gather_start(dst)
    swaps = [net.send(dst(ring.own, 64), dst(ring.own, 64), partner)]
    ring.gather_relay(dst)
    for start in (ring.last, ring.next):
        swaps.append(net.send(dst(start, 64), dst(start, 64), partner))
    ring.gather_end()
    swaps.append(net.send(dst(ring.far, 64), dst(ring.far, 64), partner))
    for copy in swaps:
        copy.wait_recv()
    net.drain()


def gram_sum(y):
    return pl.pallas_call(
        gram_kernel,
        out_shape=jax.ShapeDtypeStruct((RANK, RANK), F32),
        in_specs=[VMEM],
        out_specs=VMEM,
        scratch_shapes=ring_scratch(14, 32, 32, RANK, F32) + [pltpu.VMEM((256, RANK), F32)],
        compiler_params=params(3, 12),
        name="gram_sum",
    )(y)


def row_scatter_kernel(x_ref, o_ref, send_sems, recv_sems, got_f, got_b, sum_f, sum_b):
    net = Net(send_sems, recv_sems)
    ring, peers = row_ring(net, 1, 1)
    greet(peers)

    def src(where, count):
        return x_ref.at[pl.ds(where[1], count), pl.ds(pl.multiple_of(where[0] * 128, 128), 128)]

    send = net.send
    red = [
        send(src((ring.far, 0), 224), got_f.at[0], ring.up),
        send(src((ring.far, 224), 224), got_b.at[0], ring.down),
        send(src((ring.next, 224), 224), got_b.at[1], ring.up),
        send(src((ring.last, 0), 224), got_f.at[1], ring.down),
    ]
    red[0].wait_recv()
    sum_f[...] = (f32(got_f.at[0]) + f32(src((ring.next, 0), 224))).astype(BF16)
    red.append(send(sum_f, got_f.at[2], ring.up))
    red[1].wait_recv()
    sum_b[...] = (f32(got_b.at[0]) + f32(src((ring.last, 224), 224))).astype(BF16)
    red.append(send(sum_b, got_b.at[2], ring.down))
    for copy in red[2:]:
        copy.wait_recv()
    top = f32(src((ring.own, 0), 224)) + f32(got_f.at[1]) + f32(got_f.at[2])
    low = f32(src((ring.own, 224), 224)) + f32(got_b.at[1]) + f32(got_b.at[2])
    o_ref[pl.ds(0, 224)] = top * math.sqrt(FF)
    o_ref[pl.ds(224, 224)] = low * math.sqrt(FF)
    net.drain()


def row_scatter(x):
    return pl.pallas_call(
        row_scatter_kernel,
        out_shape=jax.ShapeDtypeStruct((COLS, RANK // 4), F32),
        in_specs=[VMEM],
        out_specs=VMEM,
        scratch_shapes=ring_scratch(6, 224, 224, 128, BF16),
        compiler_params=params(4, 8),
        name="row_scatter",
    )(x)


def unit_inverse(block):
    size, group = 128, 8
    count = size // group
    lanes = lax.broadcasted_iota(jnp.int32, (group, size), 1)
    sub = lax.broadcasted_iota(jnp.int32, (group, size), 0)

    def full(x):
        return jnp.broadcast_to(x, (group, size))

    s = [block[group * a : group * a + group] for a in range(count)]
    t = [(lanes == sub + group * a).astype(F32) for a in range(count)]
    for a in range(count):
        lo = a * group
        splat = [[full(s[b][:, lo + m : lo + m + 1]) for b in range(a, count)] for m in range(group)]
        d = [[full(splat[m][0][q : q + 1]) for m in range(group)] for q in range(group)]
        row_s = [full(s[a][q : q + 1]) for q in range(group)]
        row_t = [full(t[a][q : q + 1]) for q in range(group)]
        inv = []
        for m in range(group):
            inv.append(1.0 / d[m][m])
            for q in range(m + 1, group):
                f = d[q][m] * inv[m]
                for w in range(m + 1, group):
                    d[q][w] = d[q][w] - f * d[m][w]
                row_s[q] = row_s[q] - f * row_s[m]
                row_t[q] = row_t[q] - f * row_t[m]
        out = t[a]
        for m in range(group):
            out = jnp.where(sub == m, row_t[m] * jnp.sqrt(inv[m]), out)
        t[a] = out
        for m in reversed(range(group)):
            for q in range(m + 1, group):
                row_s[m] = row_s[m] - d[m][q] * row_s[q]
                row_t[m] = row_t[m] - d[m][q] * row_t[q]
            row_s[m] = row_s[m] * inv[m]
            row_t[m] = row_t[m] * inv[m]
        for b in range(a + 1, count):
            for m in range(group):
                s[b] = s[b] - splat[m][b - a] * row_s[m]
                t[b] = t[b] - splat[m][b - a] * row_t[m]
    return jnp.concatenate(t, axis=0)


def inverse_kernel(g_ref, high_ref, low_ref, x_ref):
    size = 128
    x_ref[...] = g_ref[...]
    eye = lax.broadcasted_iota(jnp.int32, (size, size), 0) == lax.broadcasted_iota(jnp.int32, (size, size), 1)

    def dot(a, b, dims):
        return lax.dot_general(a, b, (dims, ((), ())), precision=lax.Precision.HIGHEST, preferred_element_type=F32)

    def block(k, carry):
        at = pl.ds(pl.multiple_of(k * size, size), size)
        unit = unit_inverse(x_ref[at, at])
        x_ref[:, at] = jnp.zeros((RANK, size), F32)
        x_ref[at, at] = eye.astype(F32)
        line = dot(unit, x_ref[at, :], ((1,), (0,)))
        later = lax.broadcasted_iota(jnp.int32, (size, RANK), 1) >= (k + 1) * size
        done = jnp.where(later, 0.0, line)
        high = done.astype(BF16)
        high_ref[at, :] = high
        low_ref[at, :] = (done - high.astype(F32)).astype(BF16)
        x_ref[...] = x_ref[...] - dot(jnp.where(later, line, 0.0), line, ((0,), (0,)))
        return carry

    lax.fori_loop(0, RANK // size, block, 0)


def inverse_factor(g):
    shape = jax.ShapeDtypeStruct((RANK, RANK), BF16)
    return pl.pallas_call(
        inverse_kernel,
        out_shape=(shape, shape),
        in_specs=[VMEM],
        out_specs=(VMEM, VMEM),
        scratch_shapes=[pltpu.VMEM((RANK, RANK), F32)],
        compiler_params=pltpu.CompilerParams(vmem_limit_bytes=16 << 20),
        name="inverse_factor",
    )(g)


def contract_rows(left, right):
    return lax.dot_general(left, right, (((0,), (0,)), ((), ())), preferred_element_type=F32)


def split_dot(left, right):
    dims = (((1,), (1,)), ((), ()))
    return sum(lax.dot_general(left, term, dims, preferred_element_type=F32) for term in right)


def local(activations, out_grads, valid_len, weight, sketch):
    seq_dev, length, width = activations.shape
    col_index = lax.axis_index("col")
    positions = lax.iota(jnp.int32, length)
    raw = jnp.dot(weight, sketch, preferred_element_type=F32)
    mass = jnp.zeros((width,), F32)
    for seq in range(seq_dev):
        valid = (positions < valid_len[seq]).astype(BF16)
        grad = contract_rows(activations[seq], out_grads[seq] * valid[:, None])
        mass = mass + jnp.sum(grad * grad, axis=1)
    weighted, scale = first_sums(raw, mass.reshape(64, 128))
    projected = row_sum(contract_rows(weight, weighted).astype(BF16))
    second = col_sum(jnp.dot(weight, projected, preferred_element_type=F32), scale)
    scale = scale.reshape(ROWS, 1)
    inverse = inverse_factor(gram_sum(second))
    basis = split_dot(second, inverse)
    own = split_dot(lax.dynamic_slice_in_dim(second, col_index * 32, 32, 0), inverse)
    part = contract_rows(weight, (scale * basis).astype(BF16)).astype(BF16)
    return own * math.sqrt(DIM), row_scatter(part).T


def solution(mesh):
    placed = (
        P("row", None, None),
        P("row", None, "col"),
        P("row"),
        P("row", "col"),
        P("col", None),
    )
    return jax.shard_map(
        local,
        mesh=mesh,
        in_specs=placed,
        out_specs=(P(("row", "col"), None), P("row", "col")),
        check_vma=False,
    )
```

```python
import functools
import math

import jax
import jax.numpy as jnp
from jax import lax
from jax.experimental import pallas as pl
from jax.experimental.pallas import tpu as pltpu
from jax.sharding import PartitionSpec as P

MESH = pl.DeviceIdType.MESH
VMEM = pl.BlockSpec(memory_space=pltpu.VMEM)
F32, BF16 = jnp.float32, jnp.bfloat16
ROWS, COLS, RANK, DIM, FF = 2048, 448, 512, 8192, 28672
HALF, YCH, ZCH = 1024, 256, 32
PIECES = 4
WIDE = RANK // PIECES
ZTYPE = F32


def f32(ref):
    return ref[...].astype(F32)


def at_rows(ref, start, count, step=16):
    return ref.at[pl.ds(pl.multiple_of(start, step), count)]


class Net:
    def __init__(self, send_sems, recv_sems):
        self.send_sems, self.recv_sems, self.copies = send_sems, recv_sems, []

    def send(self, src, dst, device):
        copy = self.make(src, dst, device)
        copy.start()
        return copy

    def make(self, src, dst, device):
        slot = len(self.copies)
        copy = pltpu.make_async_remote_copy(
            src_ref=src,
            dst_ref=dst,
            send_sem=self.send_sems.at[slot],
            recv_sem=self.recv_sems.at[slot],
            device_id=device,
            device_id_type=MESH,
        )
        self.copies.append(copy)
        return copy

    def drain(self):
        for copy in self.copies:
            copy.wait_send()


def greet(peers):
    barrier = pltpu.get_barrier_semaphore()
    for peer in peers:
        pl.semaphore_signal(barrier, inc=1, device_id=peer, device_id_type=MESH)
    pl.semaphore_wait(barrier, len(peers))


def place():
    row, col = lax.axis_index("row"), lax.axis_index("col")
    return row, col, lax.rem(col, 2), lax.rem(col // 2, 8), col // 16


class Ring:
    def __init__(self, net, me, up, down, chunk, front):
        self.net, self.up, self.down, self.front, self.back = net, up, down, front, chunk - front
        self.own = me * chunk
        self.next = lax.rem(me + 1, 4) * chunk
        self.far = lax.rem(me + 2, 4) * chunk
        self.last = lax.rem(me + 3, 4) * chunk

    def reduce_start(self, src, got_f, got_b):
        send, front, back = self.net.send, self.front, self.back
        self.red = [
            send(src(self.far, front), got_f.at[0], self.up),
            send(src(self.far + front, back), got_b.at[0], self.down),
            send(src(self.next + front, back), got_b.at[1], self.up),
            send(src(self.last, front), got_f.at[1], self.down),
        ]

    def reduce_relay(self, src, got_f, got_b, sum_f, sum_b):
        send, front, back = self.net.send, self.front, self.back
        self.red[0].wait_recv()
        sum_f[...] = (f32(got_f.at[0]) + f32(src(self.next, front))).astype(sum_f.dtype)
        self.red.append(send(sum_f, got_f.at[2], self.up))
        self.red[1].wait_recv()
        sum_b[...] = (f32(got_b.at[0]) + f32(src(self.last + front, back))).astype(sum_b.dtype)
        self.red.append(send(sum_b, got_b.at[2], self.down))

    def reduce_end(self, src, got_f, got_b):
        for copy in self.red[2:]:
            copy.wait_recv()
        top = f32(src(self.own, self.front)) + f32(got_f.at[1]) + f32(got_f.at[2])
        low = f32(src(self.own + self.front, self.back)) + f32(got_b.at[1]) + f32(got_b.at[2])
        return top, low

    def gather_start(self, dst):
        whole = dst(self.own, self.front + self.back)
        self.gat = [self.net.send(whole, whole, self.up), self.net.send(whole, whole, self.down)]

    def gather_relay(self, dst):
        self.gat[0].wait_recv()
        part = dst(self.last, self.front)
        self.gat.append(self.net.send(part, part, self.up))
        self.gat[1].wait_recv()
        part = dst(self.next + self.front, self.back)
        self.gat.append(self.net.send(part, part, self.down))

    def gather_end(self):
        self.gat[2].wait_recv()
        self.gat[3].wait_recv()


def col_sum_steps(net, x_ref, o_ref, scale_ref, square, pair, mine, got_f, got_b, sum_f, sum_b, ysum, zgot):
    row, _, core, z, y = place()

    def at(yy, zz, kk):
        return (row, (yy * 8 + zz) * 2 + kk)

    partner = at(y, z, 1 - core)
    up, down = at(lax.rem(y + 1, 4), z, core), at(lax.rem(y + 3, 4), z, core)
    zpeer = [at(y, lax.rem(z + d, 8), core) for d in range(1, 8)]
    base, other = core * HALF, (1 - core) * HALF
    state = [dict() for _ in range(PIECES)]

    def cols(p):
        return pl.ds(p * WIDE, WIDE)

    def out(p, start, count):
        return o_ref.at[pl.ds(pl.multiple_of(base + start, 16), count), cols(p)]

    def src(p):
        return lambda start, count: mine.at[p, pl.ds(pl.multiple_of(start, 16), count)]

    def own_scale():
        start = base + y * YCH + z * ZCH
        line = scale_ref[pl.ds(start // 128, 1), :]
        lanes = lax.broadcasted_iota(jnp.int32, (ZCH, 128), 1)
        rows = lax.broadcasted_iota(jnp.int32, (ZCH, 128), 0)
        picked = jnp.where(lanes == rows + lax.rem(start, 128), line, 0.0)
        scale = jnp.sum(picked, axis=1, keepdims=True)
        return scale * scale if square else scale

    def s0(p):
        half = x_ref.at[pl.ds(pl.multiple_of(other, 16), HALF), cols(p)]
        state[p]["pair"] = net.send(half, pair.at[p], partner)

    def s1(p):
        state[p]["pair"].wait_recv()
        own = x_ref.at[pl.ds(pl.multiple_of(base, 16), HALF), cols(p)]
        mine[p] = (f32(own) + f32(pair.at[p])).astype(BF16)
        ring = Ring(net, y, up, down, YCH, YCH // 2)
        state[p]["ring"] = ring
        ring.reduce_start(src(p), got_f.at[p], got_b.at[p])

    def s2(p):
        state[p]["ring"].reduce_relay(src(p), got_f.at[p], got_b.at[p], sum_f.at[p], sum_b.at[p])

    def s3(p):
        top, low = state[p]["ring"].reduce_end(src(p), got_f.at[p], got_b.at[p])
        ysum[p, pl.ds(0, YCH // 2)] = top.astype(ZTYPE)
        ysum[p, pl.ds(YCH // 2, YCH // 2)] = low.astype(ZTYPE)
        state[p]["z"] = []
        for d in range(1, 8):
            part = ysum.at[p, pl.ds(pl.multiple_of(lax.rem(z + d, 8) * ZCH, 16), ZCH)]
            state[p]["z"].append(net.send(part, zgot.at[p, d - 1], zpeer[d - 1]))

    def s4(p):
        total = f32(ysum.at[p, pl.ds(pl.multiple_of(z * ZCH, 16), ZCH)])
        for d in range(7):
            state[p]["z"][d].wait_recv()
            total = total + f32(zgot.at[p, d])
        part = out(p, y * YCH + z * ZCH, ZCH)
        part[...] = (total * own_scale()).astype(BF16)
        state[p]["g"] = [net.send(part, part, peer) for peer in zpeer]

    def s5(p):
        for copy in state[p]["g"]:
            copy.wait_recv()
        ring = state[p]["ring"]
        ring.gather_start(functools.partial(out, p))
        whole = out(p, ring.own, YCH)
        state[p]["c"] = [net.send(whole, whole, partner)]

    def s6(p):
        ring = state[p]["ring"]
        ring.gather_relay(functools.partial(out, p))
        for start in (ring.last, ring.next):
            whole = out(p, start, YCH)
            state[p]["c"].append(net.send(whole, whole, partner))

    def s7(p):
        ring = state[p]["ring"]
        ring.gather_end()
        whole = out(p, ring.far, YCH)
        state[p]["c"].append(net.send(whole, whole, partner))

    def s8(p):
        for copy in state[p]["c"]:
            copy.wait_recv()

    return [s0, s1, s2, s3, s4, s5, s6, s7, s8], [partner, up, down] + zpeer


COL_COPIES = PIECES * 29
COL_SCRATCH = [
    pltpu.VMEM((PIECES, HALF, WIDE), F32),
    pltpu.VMEM((PIECES, HALF, WIDE), BF16),
    pltpu.VMEM((PIECES, 3, YCH // 2, WIDE), BF16),
    pltpu.VMEM((PIECES, 3, YCH // 2, WIDE), BF16),
    pltpu.VMEM((PIECES, YCH // 2, WIDE), BF16),
    pltpu.VMEM((PIECES, YCH // 2, WIDE), BF16),
    pltpu.VMEM((PIECES, YCH, WIDE), ZTYPE),
    pltpu.VMEM((PIECES, 7, ZCH, WIDE), ZTYPE),
]


ORDER = (0.0, 2.5, 5.0, 7.5, 14.0, 19.0, 22.0, 24.5, 26.0)
GAPS = (0.1, 1.8, 2.2, 2.2, 4.0, 4.0, 4.0, 4.0, 4.0)


def run_steps(steps, extra=()):
    events = [(ORDER[s] + GAPS[s] * p, s, p) for s in range(len(steps)) for p in range(PIECES)]
    events += [(when, -1, n) for n, (when, _) in enumerate(extra)]
    for _, s, n in sorted(events):
        if s < 0:
            extra[n][1]()
        else:
            steps[s](n)


def col_sum_kernel(x_ref, scale_ref, o_ref, send_sems, recv_sems, *scratch):
    net = Net(send_sems, recv_sems)
    steps, peers = col_sum_steps(net, x_ref, o_ref, scale_ref, False, *scratch)
    greet(peers)
    run_steps(steps)
    net.drain()


def first_kernel(x_ref, f_ref, o_ref, scale_ref, send_sems, recv_sems, fx, f1, fc, f2, fy, f3, fz, ft, fg, *scratch):
    net = Net(send_sems, recv_sems)
    steps, peers = col_sum_steps(net, x_ref, o_ref, scale_ref, True, *scratch)
    row, col, core, z, y = place()
    xpeer = [(lax.rem(row + d, 4), col) for d in range(1, 4)]
    far = (row, (lax.rem(y + 2, 4) * 8 + z) * 2 + core)
    ypeer = [peers[1], far, peers[2]]
    state = {}

    def t0():
        state["x"] = [
            net.send(at_rows(f_ref, lax.rem(row + d, 4) * 16, 16, 8), fx.at[d - 1], xpeer[d - 1])
            for d in range(1, 4)
        ]

    def t1():
        for copy in state["x"]:
            copy.wait_recv()
        f1[...] = at_rows(f_ref, row * 16, 16, 8)[...] + fx[0] + fx[1] + fx[2]
        state["c"] = net.send(f1, fc, peers[0])

    def t2():
        state["c"].wait_recv()
        f2[...] = f1[...] + fc[...]
        state["y"] = [net.send(f2, fy.at[d], ypeer[d]) for d in range(3)]

    def t3():
        for copy in state["y"]:
            copy.wait_recv()
        f3[...] = f2[...] + fy[0] + fy[1] + fy[2]
        state["z"] = [net.send(f3, fz.at[d], peers[3 + d]) for d in range(7)]

    def t4():
        total = f3[...]
        for d in range(7):
            state["z"][d].wait_recv()
            total = total + fz[d]
        scale_ref[...] = total
        ft[...] = total[0:8] + total[8:16]
        state["t"] = [net.send(ft, fg.at[d], xpeer[d]) for d in range(3)]

    def t5():
        for copy in state["t"]:
            copy.wait_recv()
        mass = jnp.sum(ft[...] + fg[0] + fg[1] + fg[2], keepdims=True)
        scale_ref[...] = jnp.sqrt(scale_ref[...] / (mass / DIM + 1e-06))

    greet(peers + [far] + xpeer)
    run_steps(steps, ((-1.0, t0), (2.6, t1), (3.9, t2), (7.0, t3), (11.5, t4), (13.9, t5)))
    net.drain()


def params(collective_id, mib):
    return pltpu.CompilerParams(
        collective_id=collective_id, has_side_effects=True, vmem_limit_bytes=mib << 20
    )


def first_sums(raw, mass):
    piece = (16, 128)
    return pl.pallas_call(
        first_kernel,
        out_shape=(jax.ShapeDtypeStruct((ROWS, RANK), BF16), jax.ShapeDtypeStruct(piece, F32)),
        in_specs=[VMEM, VMEM],
        out_specs=(VMEM, VMEM),
        scratch_shapes=[
            pltpu.SemaphoreType.DMA((COL_COPIES + 17,)),
            pltpu.SemaphoreType.DMA((COL_COPIES + 17,)),
            pltpu.VMEM((3,) + piece, F32),
            pltpu.VMEM(piece, F32),
            pltpu.VMEM(piece, F32),
            pltpu.VMEM(piece, F32),
            pltpu.VMEM((3,) + piece, F32),
            pltpu.VMEM(piece, F32),
            pltpu.VMEM((7,) + piece, F32),
            pltpu.VMEM((8, 128), F32),
            pltpu.VMEM((3, 8, 128), F32),
        ]
        + COL_SCRATCH,
        compiler_params=params(0, 28),
        name="first_sums",
    )(raw, mass)


def col_sum(x, scale):
    return pl.pallas_call(
        col_sum_kernel,
        out_shape=jax.ShapeDtypeStruct((ROWS, RANK), BF16),
        in_specs=[VMEM, VMEM],
        out_specs=VMEM,
        scratch_shapes=[
            pltpu.SemaphoreType.DMA((COL_COPIES,)),
            pltpu.SemaphoreType.DMA((COL_COPIES,)),
        ]
        + COL_SCRATCH,
        compiler_params=params(1, 28),
        name="col_sum",
    )(x, scale)


def ring_scratch(copies, front, back, width, dtype):
    return [
        pltpu.SemaphoreType.DMA((copies,)),
        pltpu.SemaphoreType.DMA((copies,)),
        pltpu.VMEM((3, front, width), dtype),
        pltpu.VMEM((3, back, width), dtype),
        pltpu.VMEM((front, width), dtype),
        pltpu.VMEM((back, width), dtype),
    ]


def row_ring(net, chunk, front):
    row, col, _, _, _ = place()
    up, down = (lax.rem(row + 1, 4), col), (lax.rem(row + 3, 4), col)
    return Ring(net, row, up, down, chunk, front), [up, down]


def row_sum_kernel(x_ref, o_ref, send_sems, recv_sems, got_f, got_b, sum_f, sum_b):
    net = Net(send_sems, recv_sems)
    ring, peers = row_ring(net, 112, 64)
    greet(peers)
    src, dst = functools.partial(at_rows, x_ref), functools.partial(at_rows, o_ref)
    ring.reduce_start(src, got_f, got_b)
    ring.reduce_relay(src, got_f, got_b, sum_f, sum_b)
    top, low = ring.reduce_end(src, got_f, got_b)
    dst(ring.own, 64)[...] = top.astype(BF16)
    dst(ring.own + 64, 48)[...] = low.astype(BF16)
    ring.gather_start(dst)
    ring.gather_relay(dst)
    ring.gather_end()
    net.drain()


def row_sum(x):
    return pl.pallas_call(
        row_sum_kernel,
        out_shape=jax.ShapeDtypeStruct((COLS, RANK), BF16),
        in_specs=[VMEM],
        out_specs=VMEM,
        scratch_shapes=ring_scratch(10, 64, 48, RANK, BF16),
        compiler_params=params(2, 8),
        name="row_sum",
    )(x)


def unit_inverse(block):
    size, group = 128, 8
    count = size // group
    lanes = lax.broadcasted_iota(jnp.int32, (group, size), 1)
    sub = lax.broadcasted_iota(jnp.int32, (group, size), 0)

    def full(x):
        return jnp.broadcast_to(x, (group, size))

    s = [block[group * a : group * a + group] for a in range(count)]
    t = [(lanes == sub + group * a).astype(F32) for a in range(count)]
    for a in range(count):
        lo = a * group
        splat = [[full(s[b][:, lo + m : lo + m + 1]) for b in range(a, count)] for m in range(group)]
        d = [[full(splat[m][0][q : q + 1]) for m in range(group)] for q in range(group)]
        row_s = [full(s[a][q : q + 1]) for q in range(group)]
        row_t = [full(t[a][q : q + 1]) for q in range(group)]
        inv = []
        for m in range(group):
            inv.append(1.0 / d[m][m])
            for q in range(m + 1, group):
                f = d[q][m] * inv[m]
                for w in range(m + 1, group):
                    d[q][w] = d[q][w] - f * d[m][w]
                row_s[q] = row_s[q] - f * row_s[m]
                row_t[q] = row_t[q] - f * row_t[m]
        out = t[a]
        for m in range(group):
            out = jnp.where(sub == m, row_t[m] * jnp.sqrt(inv[m]), out)
        t[a] = out
        for m in reversed(range(group)):
            for q in range(m + 1, group):
                row_s[m] = row_s[m] - d[m][q] * row_s[q]
                row_t[m] = row_t[m] - d[m][q] * row_t[q]
            row_s[m] = row_s[m] * inv[m]
            row_t[m] = row_t[m] * inv[m]
        for b in range(a + 1, count):
            for m in range(group):
                s[b] = s[b] - splat[m][b - a] * row_s[m]
                t[b] = t[b] - splat[m][b - a] * row_t[m]
    return jnp.concatenate(t, axis=0)


def dot(a, b, dims, precision=None):
    return lax.dot_general(a, b, (dims, ((), ())), precision=precision, preferred_element_type=F32)


def tail_kernel(
    y_ref, scaled_ref, basis_ref, coef_ref, send_sems, recv_sems, got_f, got_b, sum_f, sum_b, own, g_ref, x_ref, m_ref, part, got, whole
):
    exact = lax.Precision.HIGHEST
    net = Net(send_sems, recv_sems)
    row, col, core, z, y = place()
    partner = (row, (y * 8 + z) * 2 + 1 - core)
    ring, peers = row_ring(net, 64, 32)
    far = (lax.rem(row + 2, 4), col)
    half = core * 256
    left = y_ref[:, pl.ds(pl.multiple_of(half, 128), 256)]
    own[...] = dot(left, y_ref[...], ((0,), (0,)))
    greet(peers + [far, partner])
    src = functools.partial(at_rows, own, step=8)

    def dst(start, count):
        return at_rows(g_ref, half + start, count, 8)

    ring.reduce_start(src, got_f, got_b)
    part[...] = dot(scaled_ref[...], y_ref[...], ((1,), (0,)))
    ring.reduce_relay(src, got_f, got_b, sum_f, sum_b)
    top, low = ring.reduce_end(src, got_f, got_b)
    dst(ring.own, 32)[...] = top
    dst(ring.own + 32, 32)[...] = low
    ring.gather_start(dst)
    swaps = [net.send(dst(ring.own, 64), dst(ring.own, 64), partner)]
    ring.gather_relay(dst)
    for start in (ring.last, ring.next):
        swaps.append(net.send(dst(start, 64), dst(start, 64), partner))
    ring.gather_end()
    swaps.append(net.send(dst(ring.far, 64), dst(ring.far, 64), partner))

    chunk = COLS // 4
    xpeer = [peers[0], far, peers[1]]
    for d in range(3):
        net.send(at_rows(part, lax.rem(row + d + 1, 4) * chunk, chunk), got.at[d], xpeer[d])
    scatter = net.copies[-3:]
    mine, summed = at_rows(part, row * chunk, chunk), at_rows(whole, row * chunk, chunk)
    gather = [net.make(summed, summed, peer) for peer in xpeer]
    for copy in swaps:
        copy.wait_recv()
    x_ref[...] = g_ref[...]

    size = 128
    eye = lax.broadcasted_iota(jnp.int32, (size, size), 0) == lax.broadcasted_iota(jnp.int32, (size, size), 1)

    def block(k, carry):
        at = pl.ds(pl.multiple_of(k * size, size), size)
        unit = unit_inverse(x_ref[at, at])
        x_ref[:, at] = jnp.zeros((RANK, size), F32)
        x_ref[at, at] = eye.astype(F32)
        line = dot(unit, x_ref[at, :], ((1,), (0,)), exact)
        later = lax.broadcasted_iota(jnp.int32, (size, RANK), 1) >= (k + 1) * size
        m_ref[at, :] = jnp.where(later, 0.0, line)
        x_ref[...] = x_ref[...] - dot(jnp.where(later, line, 0.0), line, ((0,), (0,)), exact)

        @pl.when(k == 1)
        def _():
            for copy in scatter:
                copy.wait_recv()
            summed[...] = mine[...] + got[0] + got[1] + got[2]
            for copy in gather:
                copy.start()

        return carry

    lax.fori_loop(0, RANK // size, block, 0)
    rows = y_ref[pl.ds(pl.multiple_of(col * 32, 16), 32)].astype(F32)
    basis_ref[...] = dot(rows, m_ref[...], ((1,), (1,)), exact) * math.sqrt(DIM)
    for copy in gather:
        copy.wait_recv()
    mine_rows = m_ref[pl.ds(pl.multiple_of(row * 128, 128), 128)]
    coef_ref[...] = dot(whole[...], mine_rows, ((1,), (1,)), exact) * math.sqrt(FF)
    net.drain()


def outputs(second, scaled):
    return pl.pallas_call(
        tail_kernel,
        out_shape=(jax.ShapeDtypeStruct((32, RANK), F32), jax.ShapeDtypeStruct((COLS, RANK // 4), F32)),
        in_specs=[VMEM, VMEM],
        out_specs=(VMEM, VMEM),
        scratch_shapes=ring_scratch(20, 32, 32, RANK, F32)
        + [
            pltpu.VMEM((256, RANK), F32),
            pltpu.VMEM((RANK, RANK), F32),
            pltpu.VMEM((RANK, RANK), F32),
            pltpu.VMEM((RANK, RANK), F32),
            pltpu.VMEM((COLS, RANK), F32),
            pltpu.VMEM((3, COLS // 4, RANK), F32),
            pltpu.VMEM((COLS, RANK), F32),
        ],
        compiler_params=params(3, 24),
        name="outputs",
    )(second, scaled)


def contract_rows(left, right):
    return lax.dot_general(left, right, (((0,), (0,)), ((), ())), preferred_element_type=F32)


def local(activations, out_grads, valid_len, weight, sketch):
    seq_dev, length, width = activations.shape
    positions = lax.iota(jnp.int32, length)
    raw = jnp.dot(weight, sketch, preferred_element_type=F32)
    mass = jnp.zeros((width,), F32)
    for seq in range(seq_dev):
        valid = (positions < valid_len[seq]).astype(BF16)
        grad = contract_rows(activations[seq], out_grads[seq] * valid[:, None])
        mass = mass + jnp.sum(grad * grad, axis=1)
    weighted, scale = first_sums(raw, mass.reshape(64, 128))
    projected = row_sum(contract_rows(weight, weighted).astype(BF16))
    second = col_sum(jnp.dot(weight, projected, preferred_element_type=F32), scale)
    scaled = (weight.T.astype(F32) * scale.reshape(1, ROWS)).astype(BF16)
    basis, coeffs = outputs(second, scaled)
    return basis, coeffs.T


def solution(mesh):
    placed = (
        P("row", None, None),
        P("row", None, "col"),
        P("row"),
        P("row", "col"),
        P("col", None),
    )
    return jax.shard_map(
        local,
        mesh=mesh,
        in_specs=placed,
        out_specs=(P(("row", "col"), None), P("row", "col")),
        check_vma=False,
    )
```

```python
import functools
import math

import jax
import jax.numpy as jnp
from jax import lax
from jax.experimental import pallas as pl
from jax.experimental.pallas import tpu as pltpu
from jax.sharding import PartitionSpec as P

MESH = pl.DeviceIdType.MESH
VMEM = pl.BlockSpec(memory_space=pltpu.VMEM)
F32, BF16 = jnp.float32, jnp.bfloat16
ROWS, COLS, RANK, DIM, FF = 2048, 448, 512, 8192, 28672
HALF, YCH, ZCH = 1024, 256, 32
PIECES = 4
WIDE = RANK // PIECES
ZTYPE = F32


def f32(ref):
    return ref[...].astype(F32)


def at_rows(ref, start, count, step=16):
    return ref.at[pl.ds(pl.multiple_of(start, step), count)]


class Net:
    def __init__(self, send_sems, recv_sems):
        self.send_sems, self.recv_sems, self.copies = send_sems, recv_sems, []

    def send(self, src, dst, device):
        copy = self.make(src, dst, device)
        copy.start()
        return copy

    def make(self, src, dst, device):
        slot = len(self.copies)
        copy = pltpu.make_async_remote_copy(
            src_ref=src,
            dst_ref=dst,
            send_sem=self.send_sems.at[slot],
            recv_sem=self.recv_sems.at[slot],
            device_id=device,
            device_id_type=MESH,
        )
        self.copies.append(copy)
        return copy

    def drain(self):
        for copy in self.copies:
            copy.wait_send()


def greet(peers):
    barrier = pltpu.get_barrier_semaphore()
    for peer in peers:
        pl.semaphore_signal(barrier, inc=1, device_id=peer, device_id_type=MESH)
    pl.semaphore_wait(barrier, len(peers))


def place():
    row, col = lax.axis_index("row"), lax.axis_index("col")
    return row, col, lax.rem(col, 2), lax.rem(col // 2, 8), col // 16


class Ring:
    def __init__(self, net, me, up, down, chunk, front):
        self.net, self.up, self.down, self.front, self.back = net, up, down, front, chunk - front
        self.own = me * chunk
        self.next = lax.rem(me + 1, 4) * chunk
        self.far = lax.rem(me + 2, 4) * chunk
        self.last = lax.rem(me + 3, 4) * chunk

    def reduce_start(self, src, got_f, got_b):
        send, front, back = self.net.send, self.front, self.back
        self.red = [
            send(src(self.far, front), got_f.at[0], self.up),
            send(src(self.far + front, back), got_b.at[0], self.down),
            send(src(self.next + front, back), got_b.at[1], self.up),
            send(src(self.last, front), got_f.at[1], self.down),
        ]

    def reduce_relay(self, src, got_f, got_b, sum_f, sum_b):
        send, front, back = self.net.send, self.front, self.back
        self.red[0].wait_recv()
        sum_f[...] = (f32(got_f.at[0]) + f32(src(self.next, front))).astype(sum_f.dtype)
        self.red.append(send(sum_f, got_f.at[2], self.up))
        self.red[1].wait_recv()
        sum_b[...] = (f32(got_b.at[0]) + f32(src(self.last + front, back))).astype(sum_b.dtype)
        self.red.append(send(sum_b, got_b.at[2], self.down))

    def reduce_end(self, src, got_f, got_b):
        for copy in self.red[2:]:
            copy.wait_recv()
        top = f32(src(self.own, self.front)) + f32(got_f.at[1]) + f32(got_f.at[2])
        low = f32(src(self.own + self.front, self.back)) + f32(got_b.at[1]) + f32(got_b.at[2])
        return top, low

    def gather_start(self, dst):
        whole = dst(self.own, self.front + self.back)
        self.gat = [self.net.send(whole, whole, self.up), self.net.send(whole, whole, self.down)]

    def gather_relay(self, dst):
        self.gat[0].wait_recv()
        part = dst(self.last, self.front)
        self.gat.append(self.net.send(part, part, self.up))
        self.gat[1].wait_recv()
        part = dst(self.next + self.front, self.back)
        self.gat.append(self.net.send(part, part, self.down))

    def gather_end(self):
        self.gat[2].wait_recv()
        self.gat[3].wait_recv()


def col_sum_steps(net, x_ref, o_ref, rescale, pair, mine, got_f, got_b, sum_f, sum_b, ysum, zgot):
    row, _, core, z, y = place()

    def at(yy, zz, kk):
        return (row, (yy * 8 + zz) * 2 + kk)

    partner = at(y, z, 1 - core)
    up, down = at(lax.rem(y + 1, 4), z, core), at(lax.rem(y + 3, 4), z, core)
    zpeer = [at(y, lax.rem(z + d, 8), core) for d in range(1, 8)]
    base, other = core * HALF, (1 - core) * HALF
    state = [dict() for _ in range(PIECES)]

    def cols(p):
        return pl.ds(p * WIDE, WIDE)

    def out(p, start, count):
        return o_ref.at[pl.ds(pl.multiple_of(base + start, 16), count), cols(p)]

    def src(p):
        return lambda start, count: mine.at[p, pl.ds(pl.multiple_of(start, 16), count)]

    def s0(p):
        half = x_ref.at[pl.ds(pl.multiple_of(other, 16), HALF), cols(p)]
        state[p]["pair"] = net.send(half, pair.at[p], partner)

    def s1(p):
        state[p]["pair"].wait_recv()
        own = x_ref.at[pl.ds(pl.multiple_of(base, 16), HALF), cols(p)]
        mine[p] = (f32(own) + f32(pair.at[p])).astype(BF16)
        ring = Ring(net, y, up, down, YCH, YCH // 2)
        state[p]["ring"] = ring
        ring.reduce_start(src(p), got_f.at[p], got_b.at[p])

    def s2(p):
        state[p]["ring"].reduce_relay(src(p), got_f.at[p], got_b.at[p], sum_f.at[p], sum_b.at[p])

    def s3(p):
        top, low = state[p]["ring"].reduce_end(src(p), got_f.at[p], got_b.at[p])
        ysum[p, pl.ds(0, YCH // 2)] = top.astype(ZTYPE)
        ysum[p, pl.ds(YCH // 2, YCH // 2)] = low.astype(ZTYPE)
        state[p]["z"] = []
        for d in range(1, 8):
            part = ysum.at[p, pl.ds(pl.multiple_of(lax.rem(z + d, 8) * ZCH, 16), ZCH)]
            state[p]["z"].append(net.send(part, zgot.at[p, d - 1], zpeer[d - 1]))

    def s4(p):
        total = f32(ysum.at[p, pl.ds(pl.multiple_of(z * ZCH, 16), ZCH)])
        for d in range(7):
            state[p]["z"][d].wait_recv()
            total = total + f32(zgot.at[p, d])
        part = out(p, y * YCH + z * ZCH, ZCH)
        part[...] = rescale(total, base + y * YCH + z * ZCH).astype(BF16)
        state[p]["g"] = [net.send(part, part, peer) for peer in zpeer]

    def s5(p):
        for copy in state[p]["g"]:
            copy.wait_recv()
        ring = state[p]["ring"]
        ring.gather_start(functools.partial(out, p))
        whole = out(p, ring.own, YCH)
        state[p]["c"] = [net.send(whole, whole, partner)]

    def s6(p):
        ring = state[p]["ring"]
        ring.gather_relay(functools.partial(out, p))
        for start in (ring.last, ring.next):
            whole = out(p, start, YCH)
            state[p]["c"].append(net.send(whole, whole, partner))

    def s7(p):
        ring = state[p]["ring"]
        ring.gather_end()
        whole = out(p, ring.far, YCH)
        state[p]["c"].append(net.send(whole, whole, partner))

    def s8(p):
        for copy in state[p]["c"]:
            copy.wait_recv()

    return [s0, s1, s2, s3, s4, s5, s6, s7, s8], [partner, up, down] + zpeer


COL_SCRATCH = [
    pltpu.VMEM((PIECES, HALF, WIDE), F32),
    pltpu.VMEM((PIECES, HALF, WIDE), BF16),
    pltpu.VMEM((PIECES, 3, YCH // 2, WIDE), BF16),
    pltpu.VMEM((PIECES, 3, YCH // 2, WIDE), BF16),
    pltpu.VMEM((PIECES, YCH // 2, WIDE), BF16),
    pltpu.VMEM((PIECES, YCH // 2, WIDE), BF16),
    pltpu.VMEM((PIECES, YCH, WIDE), ZTYPE),
    pltpu.VMEM((PIECES, 7, ZCH, WIDE), ZTYPE),
]


LINK = (0.0, 2.5, 5.0, 7.5, 14.0, 19.0, 22.0, 24.5, 26.0)
TURN = (26.2, 28.8, 31.0, 33.5, 36.0)
ORDER = LINK + TURN + tuple(36.5 + t for t in LINK)
GAPS = (0.1, 1.8, 2.2, 2.2) + (4.5,) * 19


def run_steps(steps, extra=()):
    events = [(ORDER[s] + GAPS[s] * p, s, p) for s in range(len(steps)) for p in range(PIECES)]
    events += [(when, -1, n) for n, (when, _) in enumerate(extra)]
    for _, s, n in sorted(events):
        if s < 0:
            extra[n][1]()
        else:
            steps[s](n)


def fisher_steps(net, f_ref, scale_ref, peers, far, xpeer, fx, f1, fc, f2, fy, f3, fz, ft, fg):
    row = lax.axis_index("row")
    ypeer = [peers[1], far, peers[2]]
    state = {}

    def t0():
        state["x"] = [
            net.send(at_rows(f_ref, lax.rem(row + d, 4) * 16, 16, 8), fx.at[d - 1], xpeer[d - 1])
            for d in range(1, 4)
        ]

    def t1():
        for copy in state["x"]:
            copy.wait_recv()
        f1[...] = at_rows(f_ref, row * 16, 16, 8)[...] + fx[0] + fx[1] + fx[2]
        state["c"] = net.send(f1, fc, peers[0])

    def t2():
        state["c"].wait_recv()
        f2[...] = f1[...] + fc[...]
        state["y"] = [net.send(f2, fy.at[d], ypeer[d]) for d in range(3)]

    def t3():
        for copy in state["y"]:
            copy.wait_recv()
        f3[...] = f2[...] + fy[0] + fy[1] + fy[2]
        state["z"] = [net.send(f3, fz.at[d], peers[3 + d]) for d in range(7)]

    def t4():
        total = f3[...]
        for d in range(7):
            state["z"][d].wait_recv()
            total = total + fz[d]
        scale_ref[...] = total
        ft[...] = total[0:8] + total[8:16]
        state["t"] = [net.send(ft, fg.at[d], xpeer[d]) for d in range(3)]

    def t5():
        for copy in state["t"]:
            copy.wait_recv()
        mass = jnp.sum(ft[...] + fg[0] + fg[1] + fg[2], keepdims=True)
        scale_ref[...] = jnp.sqrt(scale_ref[...] / (mass / DIM + 1e-06))

    return [t0, t1, t2, t3, t4, t5]


def chain_kernel(
    x_ref, f_ref, weight_ref, y_ref, scaled_ref, send_sems, recv_sems, scale_ref, first, back, again, part, xgot_f, xgot_b,
    xsum_f, xsum_b, projected, *scratch
):
    net = Net(send_sems, recv_sems)
    row, col, core, z, y = place()

    def rescale(total, start):
        line = scale_ref[pl.ds(start // 128, 1), :]
        lanes = lax.broadcasted_iota(jnp.int32, (ZCH, 128), 1)
        rows = lax.broadcasted_iota(jnp.int32, (ZCH, 128), 0)
        picked = jnp.where(lanes == rows + lax.rem(start, 128), line, 0.0)
        return total * jnp.sum(picked, axis=1, keepdims=True)

    sum1, peers = col_sum_steps(net, x_ref, first, rescale, *scratch[:8])
    sum2, _ = col_sum_steps(net, again, y_ref, lambda total, start: total, *scratch[8:16])
    xpeer = [(lax.rem(row + d, 4), col) for d in range(1, 4)]
    far = (row, (lax.rem(y + 2, 4) * 8 + z) * 2 + core)
    fisher = fisher_steps(net, f_ref, scale_ref, peers, far, xpeer, *scratch[16:])
    rings = [Ring(net, row, xpeer[0], xpeer[2], COLS // 4, 64) for _ in range(PIECES)]

    def scale_weight(n):
        def step():
            for b in range(4 * n, 4 * n + 4):
                at = pl.ds(b * 128, 128)
                block = weight_ref[:, at].astype(F32) * scale_ref[b : b + 1, :]
                scaled_ref[:, at] = block.astype(BF16)
                back[at, :] = block.T.astype(BF16)

        return step

    def src(p):
        return lambda start, count: at_rows(part.at[p], start, count)

    def dst(p):
        return lambda start, count: at_rows(projected.at[p], start, count)

    def q0(p):
        part[p] = dot(scaled_ref[...], first[:, pl.ds(p * WIDE, WIDE)], ((1,), (0,))).astype(BF16)
        rings[p].reduce_start(src(p), xgot_f.at[p], xgot_b.at[p])

    def q1(p):
        rings[p].reduce_relay(src(p), xgot_f.at[p], xgot_b.at[p], xsum_f.at[p], xsum_b.at[p])

    def q2(p):
        top, low = rings[p].reduce_end(src(p), xgot_f.at[p], xgot_b.at[p])
        dst(p)(rings[p].own, 64)[...] = top.astype(BF16)
        dst(p)(rings[p].own + 64, 48)[...] = low.astype(BF16)
        rings[p].gather_start(dst(p))

    def q3(p):
        rings[p].gather_relay(dst(p))

    def q4(p):
        rings[p].gather_end()
        again[:, pl.ds(p * WIDE, WIDE)] = dot(back[...], projected[p], ((1,), (0,)))

    greet(peers + [far] + xpeer)
    extra = list(zip((-1.0, 2.6, 3.9, 7.0, 11.5, 13.9), fisher))
    extra += [(when, scale_weight(n)) for n, when in enumerate((14.5, 18.0, 20.0, 23.0))]
    run_steps(sum1 + [q0, q1, q2, q3, q4] + sum2, extra)
    net.drain()


def params(collective_id, mib):
    return pltpu.CompilerParams(
        collective_id=collective_id, has_side_effects=True, vmem_limit_bytes=mib << 20
    )


def chain(raw, mass, weight):
    piece = (16, 128)
    copies = PIECES * 68 + 17
    return pl.pallas_call(
        chain_kernel,
        out_shape=(jax.ShapeDtypeStruct((ROWS, RANK), BF16), jax.ShapeDtypeStruct((COLS, ROWS), BF16)),
        in_specs=[VMEM, VMEM, VMEM],
        out_specs=(VMEM, VMEM),
        scratch_shapes=[
            pltpu.SemaphoreType.DMA((copies,)),
            pltpu.SemaphoreType.DMA((copies,)),
            pltpu.VMEM(piece, F32),
            pltpu.VMEM((ROWS, RANK), BF16),
            pltpu.VMEM((ROWS, COLS), BF16),
            pltpu.VMEM((ROWS, RANK), F32),
            pltpu.VMEM((PIECES, COLS, WIDE), BF16),
            pltpu.VMEM((PIECES, 3, 64, WIDE), BF16),
            pltpu.VMEM((PIECES, 3, 48, WIDE), BF16),
            pltpu.VMEM((PIECES, 64, WIDE), BF16),
            pltpu.VMEM((PIECES, 48, WIDE), BF16),
            pltpu.VMEM((PIECES, COLS, WIDE), BF16),
        ]
        + COL_SCRATCH
        + COL_SCRATCH
        + [
            pltpu.VMEM((3,) + piece, F32),
            pltpu.VMEM(piece, F32),
            pltpu.VMEM(piece, F32),
            pltpu.VMEM(piece, F32),
            pltpu.VMEM((3,) + piece, F32),
            pltpu.VMEM(piece, F32),
            pltpu.VMEM((7,) + piece, F32),
            pltpu.VMEM((8, 128), F32),
            pltpu.VMEM((3, 8, 128), F32),
        ],
        compiler_params=params(0, 44),
        name="chain",
    )(raw, mass, weight)


def ring_scratch(copies, front, back, width, dtype):
    return [
        pltpu.SemaphoreType.DMA((copies,)),
        pltpu.SemaphoreType.DMA((copies,)),
        pltpu.VMEM((3, front, width), dtype),
        pltpu.VMEM((3, back, width), dtype),
        pltpu.VMEM((front, width), dtype),
        pltpu.VMEM((back, width), dtype),
    ]


def row_ring(net, chunk, front):
    row, col, _, _, _ = place()
    up, down = (lax.rem(row + 1, 4), col), (lax.rem(row + 3, 4), col)
    return Ring(net, row, up, down, chunk, front), [up, down]


def unit_inverse(block):
    size, group = 128, 8
    count = size // group
    lanes = lax.broadcasted_iota(jnp.int32, (group, size), 1)
    sub = lax.broadcasted_iota(jnp.int32, (group, size), 0)

    def full(x):
        return jnp.broadcast_to(x, (group, size))

    s = [block[group * a : group * a + group] for a in range(count)]
    t = [(lanes == sub + group * a).astype(F32) for a in range(count)]
    for a in range(count):
        lo = a * group
        splat = [[full(s[b][:, lo + m : lo + m + 1]) for b in range(a, count)] for m in range(group)]
        d = [[full(splat[m][0][q : q + 1]) for m in range(group)] for q in range(group)]
        row_s = [full(s[a][q : q + 1]) for q in range(group)]
        row_t = [full(t[a][q : q + 1]) for q in range(group)]
        inv = []
        for m in range(group):
            inv.append(1.0 / d[m][m])
            for q in range(m + 1, group):
                f = d[q][m] * inv[m]
                for w in range(m + 1, group):
                    d[q][w] = d[q][w] - f * d[m][w]
                row_s[q] = row_s[q] - f * row_s[m]
                row_t[q] = row_t[q] - f * row_t[m]
        out = t[a]
        for m in range(group):
            out = jnp.where(sub == m, row_t[m] * jnp.sqrt(inv[m]), out)
        t[a] = out
        for m in reversed(range(group)):
            for q in range(m + 1, group):
                row_s[m] = row_s[m] - d[m][q] * row_s[q]
                row_t[m] = row_t[m] - d[m][q] * row_t[q]
            row_s[m] = row_s[m] * inv[m]
            row_t[m] = row_t[m] * inv[m]
        for b in range(a + 1, count):
            for m in range(group):
                s[b] = s[b] - splat[m][b - a] * row_s[m]
                t[b] = t[b] - splat[m][b - a] * row_t[m]
    return jnp.concatenate(t, axis=0)


def dot(a, b, dims, precision=None):
    return lax.dot_general(a, b, (dims, ((), ())), precision=precision, preferred_element_type=F32)


def tail_kernel(
    y_ref, scaled_ref, basis_ref, coef_ref, send_sems, recv_sems, got_f, got_b, sum_f, sum_b, own, g_ref, x_ref, m_ref, part, got, whole
):
    exact = lax.Precision.HIGHEST
    net = Net(send_sems, recv_sems)
    row, col, core, z, y = place()
    partner = (row, (y * 8 + z) * 2 + 1 - core)
    ring, peers = row_ring(net, 64, 32)
    far = (lax.rem(row + 2, 4), col)
    half = core * 256
    left = y_ref[:, pl.ds(pl.multiple_of(half, 128), 256)]
    own[...] = dot(left, y_ref[...], ((0,), (0,)))
    greet(peers + [far, partner])
    src = functools.partial(at_rows, own, step=8)

    def dst(start, count):
        return at_rows(g_ref, half + start, count, 8)

    ring.reduce_start(src, got_f, got_b)
    part[...] = dot(scaled_ref[...], y_ref[...], ((1,), (0,)))
    ring.reduce_relay(src, got_f, got_b, sum_f, sum_b)
    top, low = ring.reduce_end(src, got_f, got_b)
    dst(ring.own, 32)[...] = top
    dst(ring.own + 32, 32)[...] = low
    ring.gather_start(dst)
    swaps = [net.send(dst(ring.own, 64), dst(ring.own, 64), partner)]
    ring.gather_relay(dst)
    for start in (ring.last, ring.next):
        swaps.append(net.send(dst(start, 64), dst(start, 64), partner))
    ring.gather_end()
    swaps.append(net.send(dst(ring.far, 64), dst(ring.far, 64), partner))

    chunk = COLS // 4
    xpeer = [peers[0], far, peers[1]]
    for d in range(3):
        net.send(at_rows(part, lax.rem(row + d + 1, 4) * chunk, chunk), got.at[d], xpeer[d])
    scatter = net.copies[-3:]
    mine, summed = at_rows(part, row * chunk, chunk), at_rows(whole, row * chunk, chunk)
    gather = [net.make(summed, summed, peer) for peer in xpeer]
    for copy in swaps:
        copy.wait_recv()
    x_ref[...] = g_ref[...]

    size = 128
    eye = lax.broadcasted_iota(jnp.int32, (size, size), 0) == lax.broadcasted_iota(jnp.int32, (size, size), 1)

    def block(k, carry):
        at = pl.ds(pl.multiple_of(k * size, size), size)
        unit = unit_inverse(x_ref[at, at])
        x_ref[:, at] = jnp.zeros((RANK, size), F32)
        x_ref[at, at] = eye.astype(F32)
        line = dot(unit, x_ref[at, :], ((1,), (0,)), exact)
        later = lax.broadcasted_iota(jnp.int32, (size, RANK), 1) >= (k + 1) * size
        m_ref[at, :] = jnp.where(later, 0.0, line)
        x_ref[...] = x_ref[...] - dot(jnp.where(later, line, 0.0), line, ((0,), (0,)), exact)

        @pl.when(k == 1)
        def _():
            for copy in scatter:
                copy.wait_recv()
            summed[...] = mine[...] + got[0] + got[1] + got[2]
            for copy in gather:
                copy.start()

        return carry

    lax.fori_loop(0, RANK // size, block, 0)
    rows = y_ref[pl.ds(pl.multiple_of(col * 32, 16), 32)].astype(F32)
    basis_ref[...] = dot(rows, m_ref[...], ((1,), (1,)), exact) * math.sqrt(DIM)
    for copy in gather:
        copy.wait_recv()
    mine_rows = m_ref[pl.ds(pl.multiple_of(row * 128, 128), 128)]
    coef_ref[...] = dot(whole[...], mine_rows, ((1,), (1,)), exact) * math.sqrt(FF)
    net.drain()


def outputs(second, scaled):
    return pl.pallas_call(
        tail_kernel,
        out_shape=(jax.ShapeDtypeStruct((32, RANK), F32), jax.ShapeDtypeStruct((COLS, RANK // 4), F32)),
        in_specs=[VMEM, VMEM],
        out_specs=(VMEM, VMEM),
        scratch_shapes=ring_scratch(20, 32, 32, RANK, F32)
        + [
            pltpu.VMEM((256, RANK), F32),
            pltpu.VMEM((RANK, RANK), F32),
            pltpu.VMEM((RANK, RANK), F32),
            pltpu.VMEM((RANK, RANK), F32),
            pltpu.VMEM((COLS, RANK), F32),
            pltpu.VMEM((3, COLS // 4, RANK), F32),
            pltpu.VMEM((COLS, RANK), F32),
        ],
        compiler_params=params(3, 24),
        name="outputs",
    )(second, scaled)


def contract_rows(left, right):
    return lax.dot_general(left, right, (((0,), (0,)), ((), ())), preferred_element_type=F32)


def local(activations, out_grads, valid_len, weight, sketch):
    seq_dev, length, width = activations.shape
    positions = lax.iota(jnp.int32, length)
    raw = jnp.dot(weight, sketch, preferred_element_type=F32)
    mass = jnp.zeros((width,), F32)
    for seq in range(seq_dev):
        valid = (positions < valid_len[seq]).astype(BF16)
        grad = contract_rows(activations[seq], out_grads[seq] * valid[:, None])
        mass = mass + jnp.sum(grad * grad, axis=1)
    second, scaled = chain(raw, mass.reshape(64, 128), weight.T)
    basis, coeffs = outputs(second, scaled)
    return basis, coeffs.T


def solution(mesh):
    placed = (
        P("row", None, None),
        P("row", None, "col"),
        P("row"),
        P("row", "col"),
        P("col", None),
    )
    return jax.shard_map(
        local,
        mesh=mesh,
        in_specs=placed,
        out_specs=(P(("row", "col"), None), P("row", "col")),
        check_vma=False,
    )
```

```python
import functools
import math

import jax
import jax.numpy as jnp
from jax import lax
from jax.experimental import pallas as pl
from jax.experimental.pallas import tpu as pltpu
from jax.sharding import PartitionSpec as P

MESH = pl.DeviceIdType.MESH
VMEM = pl.BlockSpec(memory_space=pltpu.VMEM)
F32, BF16 = jnp.float32, jnp.bfloat16
ROWS, COLS, RANK, DIM, FF = 2048, 448, 512, 8192, 28672
HALF, YCH, ZCH, LEN = 1024, 256, 32, 256
PIECES = 4
WIDE = RANK // PIECES
ZTYPE = BF16


def f32(ref):
    return ref[...].astype(F32)


def at_rows(ref, start, count, step=16):
    return ref.at[pl.ds(pl.multiple_of(start, step), count)]


class Net:
    def __init__(self, send_sems, recv_sems):
        self.send_sems, self.recv_sems, self.copies = send_sems, recv_sems, []

    def send(self, src, dst, device):
        copy = self.make(src, dst, device)
        copy.start()
        return copy

    def make(self, src, dst, device):
        slot = len(self.copies)
        copy = pltpu.make_async_remote_copy(
            src_ref=src,
            dst_ref=dst,
            send_sem=self.send_sems.at[slot],
            recv_sem=self.recv_sems.at[slot],
            device_id=device,
            device_id_type=MESH,
        )
        self.copies.append(copy)
        return copy

    def drain(self):
        for copy in self.copies:
            copy.wait_send()


def greet(peers):
    barrier = pltpu.get_barrier_semaphore()
    for peer in peers:
        pl.semaphore_signal(barrier, inc=1, device_id=peer, device_id_type=MESH)
    return lambda: pl.semaphore_wait(barrier, len(peers))


def place():
    row, col = lax.axis_index("row"), lax.axis_index("col")
    return row, col, lax.rem(col, 2), lax.rem(col // 2, 8), col // 16


class Ring:
    def __init__(self, net, me, up, down, chunk, front):
        self.net, self.up, self.down, self.front, self.back = net, up, down, front, chunk - front
        self.own = me * chunk
        self.next = lax.rem(me + 1, 4) * chunk
        self.far = lax.rem(me + 2, 4) * chunk
        self.last = lax.rem(me + 3, 4) * chunk

    def reduce_start(self, src, got_f, got_b):
        send, front, back = self.net.send, self.front, self.back
        self.red = [
            send(src(self.far, front), got_f.at[0], self.up),
            send(src(self.far + front, back), got_b.at[0], self.down),
            send(src(self.next + front, back), got_b.at[1], self.up),
            send(src(self.last, front), got_f.at[1], self.down),
        ]

    def reduce_relay(self, src, got_f, got_b, sum_f, sum_b):
        send, front, back = self.net.send, self.front, self.back
        self.red[0].wait_recv()
        sum_f[...] = (f32(got_f.at[0]) + f32(src(self.next, front))).astype(sum_f.dtype)
        self.red.append(send(sum_f, got_f.at[2], self.up))
        self.red[1].wait_recv()
        sum_b[...] = (f32(got_b.at[0]) + f32(src(self.last + front, back))).astype(sum_b.dtype)
        self.red.append(send(sum_b, got_b.at[2], self.down))

    def reduce_end(self, src, got_f, got_b):
        for copy in self.red[2:]:
            copy.wait_recv()
        top = f32(src(self.own, self.front)) + f32(got_f.at[1]) + f32(got_f.at[2])
        low = f32(src(self.own + self.front, self.back)) + f32(got_b.at[1]) + f32(got_b.at[2])
        return top, low

    def gather_start(self, dst):
        whole = dst(self.own, self.front + self.back)
        self.gat = [self.net.send(whole, whole, self.up), self.net.send(whole, whole, self.down)]

    def gather_relay(self, dst):
        self.gat[0].wait_recv()
        part = dst(self.last, self.front)
        self.gat.append(self.net.send(part, part, self.up))
        self.gat[1].wait_recv()
        part = dst(self.next + self.front, self.back)
        self.gat.append(self.net.send(part, part, self.down))

    def gather_end(self):
        self.gat[2].wait_recv()
        self.gat[3].wait_recv()


def col_sum_steps(net, x_ref, o_ref, rescale, pair, mine, got_f, got_b, sum_f, sum_b, ysum, zgot):
    row, _, core, z, y = place()

    def at(yy, zz, kk):
        return (row, (yy * 8 + zz) * 2 + kk)

    partner = at(y, z, 1 - core)
    up, down = at(lax.rem(y + 1, 4), z, core), at(lax.rem(y + 3, 4), z, core)
    zpeer = [at(y, lax.rem(z + d, 8), core) for d in range(1, 8)]
    base, other = core * HALF, (1 - core) * HALF
    state = [dict() for _ in range(PIECES)]

    def cols(p):
        return pl.ds(p * WIDE, WIDE)

    def out(p, start, count):
        return o_ref.at[pl.ds(pl.multiple_of(base + start, 16), count), cols(p)]

    def src(p):
        return lambda start, count: mine.at[p, pl.ds(pl.multiple_of(start, 16), count)]

    def s0(p):
        half = x_ref.at[pl.ds(pl.multiple_of(other, 16), HALF), cols(p)]
        state[p]["pair"] = net.send(half, pair.at[p], partner)

    def s1(p):
        state[p]["pair"].wait_recv()
        own = x_ref.at[pl.ds(pl.multiple_of(base, 16), HALF), cols(p)]
        mine[p] = (f32(own) + f32(pair.at[p])).astype(BF16)
        ring = Ring(net, y, up, down, YCH, YCH // 2)
        state[p]["ring"] = ring
        ring.reduce_start(src(p), got_f.at[p], got_b.at[p])

    def s2(p):
        state[p]["ring"].reduce_relay(src(p), got_f.at[p], got_b.at[p], sum_f.at[p], sum_b.at[p])

    def s3(p):
        top, low = state[p]["ring"].reduce_end(src(p), got_f.at[p], got_b.at[p])
        ysum[p, pl.ds(0, YCH // 2)] = top.astype(ZTYPE)
        ysum[p, pl.ds(YCH // 2, YCH // 2)] = low.astype(ZTYPE)
        state[p]["z"] = []
        for d in range(1, 8):
            part = ysum.at[p, pl.ds(pl.multiple_of(lax.rem(z + d, 8) * ZCH, 16), ZCH)]
            state[p]["z"].append(net.send(part, zgot.at[p, d - 1], zpeer[d - 1]))

    def s4(p):
        total = f32(ysum.at[p, pl.ds(pl.multiple_of(z * ZCH, 16), ZCH)])
        for d in range(7):
            state[p]["z"][d].wait_recv()
            total = total + f32(zgot.at[p, d])
        part = out(p, y * YCH + z * ZCH, ZCH)
        part[...] = rescale(total, base + y * YCH + z * ZCH).astype(BF16)
        state[p]["g"] = [net.send(part, part, peer) for peer in zpeer]

    def s5(p):
        for copy in state[p]["g"]:
            copy.wait_recv()
        ring = state[p]["ring"]
        ring.gather_start(functools.partial(out, p))
        whole = out(p, ring.own, YCH)
        state[p]["c"] = [net.send(whole, whole, partner)]

    def s6(p):
        ring = state[p]["ring"]
        ring.gather_relay(functools.partial(out, p))
        for start in (ring.last, ring.next):
            whole = out(p, start, YCH)
            state[p]["c"].append(net.send(whole, whole, partner))

    def s7(p):
        ring = state[p]["ring"]
        ring.gather_end()
        whole = out(p, ring.far, YCH)
        state[p]["c"].append(net.send(whole, whole, partner))

    def s8(p):
        for copy in state[p]["c"]:
            copy.wait_recv()

    return [s0, s1, s2, s3, s4, s5, s6, s7, s8], [partner, up, down] + zpeer


COL_SCRATCH = [
    pltpu.VMEM((PIECES, HALF, WIDE), F32),
    pltpu.VMEM((PIECES, HALF, WIDE), BF16),
    pltpu.VMEM((PIECES, 3, YCH // 2, WIDE), BF16),
    pltpu.VMEM((PIECES, 3, YCH // 2, WIDE), BF16),
    pltpu.VMEM((PIECES, YCH // 2, WIDE), BF16),
    pltpu.VMEM((PIECES, YCH // 2, WIDE), BF16),
    pltpu.VMEM((PIECES, YCH, WIDE), ZTYPE),
    pltpu.VMEM((PIECES, 7, ZCH, WIDE), ZTYPE),
]


ORDER = (
    100, 4, 5, 101, 102, 8, 9, 6, 103, 7, 12, 13, 10, 14, 11, 104,
    105, 16, 17, 15, 110, 111, 112, 113, 18, 20, 21, 24, 19, 25, 22, 28,
    32, 36, 29, 26, 33, 37, 23, 40, 30, 44, 41, 27, 34, 38, 48, 31,
    45, 42, 35, 39, 52, 56, 46, 49, 43, 60, 50, 53, 57, 47, 64, 54,
    58, 61, 51, 68, 62, 65, 55, 59, 66, 63, 69, 70, 72, 67, 71, 73,
    74, 76, 75, 77, 78, 81, 80, 79, 82, 84, 83, 86, 85, 89, 90, 88,
    87, 91,
)


def run_steps(steps, fisher, weight):
    for event in ORDER:
        if event >= 110:
            weight[event - 110]()
        elif event >= 100:
            fisher[event - 100]()
        else:
            steps[event // PIECES](event % PIECES)


def fisher_steps(net, f_ref, scale_ref, peers, far, xpeer, fx, f1, fc, f2, fy, f3, fz, ft, fg):
    row = lax.axis_index("row")
    ypeer = [peers[1], far, peers[2]]
    state = {}

    def t0():
        state["x"] = [
            net.send(at_rows(f_ref, lax.rem(row + d, 4) * 16, 16, 8), fx.at[d - 1], xpeer[d - 1])
            for d in range(1, 4)
        ]

    def t1():
        for copy in state["x"]:
            copy.wait_recv()
        f1[...] = at_rows(f_ref, row * 16, 16, 8)[...] + fx[0] + fx[1] + fx[2]
        state["c"] = net.send(f1, fc, peers[0])

    def t2():
        state["c"].wait_recv()
        f2[...] = f1[...] + fc[...]
        state["y"] = [net.send(f2, fy.at[d], ypeer[d]) for d in range(3)]

    def t3():
        for copy in state["y"]:
            copy.wait_recv()
        f3[...] = f2[...] + fy[0] + fy[1] + fy[2]
        state["z"] = [net.send(f3, fz.at[d], peers[3 + d]) for d in range(7)]

    def t4():
        total = f3[...]
        for d in range(7):
            state["z"][d].wait_recv()
            total = total + fz[d]
        scale_ref[...] = total
        ft[...] = total[0:8] + total[8:16]
        state["t"] = [net.send(ft, fg.at[d], xpeer[d]) for d in range(3)]

    def t5():
        for copy in state["t"]:
            copy.wait_recv()
        mass = jnp.sum(ft[...] + fg[0] + fg[1] + fg[2], keepdims=True)
        scale_ref[...] = jnp.sqrt(jnp.maximum(scale_ref[...], 0.0) / (mass / DIM + 1e-06))

    return [t0, t1, t2, t3, t4, t5]


def chain_kernel(
    sketch_ref, acts_ref, grads_ref, len_ref, weight_ref, y_ref, scaled_ref, send_sems, recv_sems, load_sems, x_ref, acts, f_ref, scale_ref, first, back, again, part, xgot_f, xgot_b,
    xsum_f, xsum_b, projected, *scratch
):
    net = Net(send_sems, recv_sems)
    row, col, core, z, y = place()

    def rescale(total, start):
        line = scale_ref[pl.ds(start // 128, 1), :]
        lanes = lax.broadcasted_iota(jnp.int32, (ZCH, 128), 1)
        rows = lax.broadcasted_iota(jnp.int32, (ZCH, 128), 0)
        picked = jnp.where(lanes == rows + lax.rem(start, 128), line, 0.0)
        return total * jnp.sum(picked, axis=1, keepdims=True)

    sum1, peers = col_sum_steps(net, x_ref, first, rescale, *scratch[:8])
    sum2, _ = col_sum_steps(net, again, y_ref, lambda total, start: total, *scratch[8:16])
    xpeer = [(lax.rem(row + d, 4), col) for d in range(1, 4)]
    far = (row, (lax.rem(y + 2, 4) * 8 + z) * 2 + core)
    fisher = fisher_steps(net, f_ref, scale_ref, peers, far, xpeer, *scratch[16:])
    rings = [Ring(net, row, xpeer[0], xpeer[2], COLS // 4, 64) for _ in range(PIECES)]

    def scale_weight(n):
        def step():
            for b in range(4 * n, 4 * n + 4):
                at = pl.ds(b * 128, 128)
                block = weight_ref[:, at].astype(F32) * scale_ref[b : b + 1, :]
                scaled_ref[:, at] = block.astype(BF16)
                back[at, :] = block.T.astype(BF16)

        return step

    def src(p):
        return lambda start, count: at_rows(part.at[p], start, count)

    def dst(p):
        return lambda start, count: at_rows(projected.at[p], start, count)

    def q0(p):
        part[p] = dot(scaled_ref[...], first[:, pl.ds(p * WIDE, WIDE)], ((1,), (0,))).astype(BF16)
        rings[p].reduce_start(src(p), xgot_f.at[p], xgot_b.at[p])

    def q1(p):
        rings[p].reduce_relay(src(p), xgot_f.at[p], xgot_b.at[p], xsum_f.at[p], xsum_b.at[p])

    def q2(p):
        top, low = rings[p].reduce_end(src(p), xgot_f.at[p], xgot_b.at[p])
        dst(p)(rings[p].own, 64)[...] = top.astype(BF16)
        dst(p)(rings[p].own + 64, 48)[...] = low.astype(BF16)
        rings[p].gather_start(dst(p))

    def q3(p):
        rings[p].gather_relay(dst(p))

    def q4(p):
        rings[p].gather_end()
        again[:, pl.ds(p * WIDE, WIDE)] = dot(back[...], projected[p], ((1,), (0,)))

    arrived = greet(peers + [far] + xpeer)
    loads = [pltpu.make_async_copy(acts_ref.at[n], acts.at[n], load_sems.at[n]) for n in range(2)]
    for load in loads:
        load.start()
    for n in range(4):
        at = pl.ds(n * 512, 512)
        x_ref[at, :] = dot(weight_ref[:, at], sketch_ref[...], ((0,), (0,)))

    def masses(n):
        loads[n].wait()
        valid = lax.broadcasted_iota(jnp.int32, (COLS, LEN), 1) < len_ref[n]
        grads = jnp.where(valid, grads_ref[n].astype(F32), 0.0).astype(BF16)
        tokens = dot(grads, grads, ((0,), (0,)))
        high = tokens.astype(BF16)
        low = (tokens - high.astype(F32)).astype(BF16)
        for c in range(8):
            block = acts[n, :, pl.ds(c * 1024, 1024)]
            mixed = dot(high, block, ((1,), (0,))) + dot(low, block, ((1,), (0,)))
            sums = jnp.sum(block.astype(F32) * mixed, axis=0, keepdims=True)
            for i in range(8):
                at = pl.ds(8 * c + i, 1)
                line = sums[:, i * 128 : (i + 1) * 128]
                f_ref[at, :] = line if n == 0 else f_ref[at, :] + line

    masses(0)
    arrived()
    for p in range(PIECES):
        sum1[0](p)
    masses(1)
    run_steps(sum1 + [q0, q1, q2, q3, q4] + sum2, fisher, [scale_weight(n) for n in range(4)])
    net.drain()


def params(collective_id, mib):
    return pltpu.CompilerParams(
        collective_id=collective_id, has_side_effects=True, vmem_limit_bytes=mib << 20
    )


def chain(sketch, acts, grads, lens, weight):
    piece = (16, 128)
    copies = PIECES * 68 + 17
    return pl.pallas_call(
        chain_kernel,
        out_shape=(jax.ShapeDtypeStruct((ROWS, RANK), BF16), jax.ShapeDtypeStruct((COLS, ROWS), BF16)),
        in_specs=[
            VMEM,
            pl.BlockSpec(memory_space=pltpu.HBM),
            VMEM,
            pl.BlockSpec(memory_space=pltpu.SMEM),
            VMEM,
        ],
        out_specs=(VMEM, VMEM),
        scratch_shapes=[
            pltpu.SemaphoreType.DMA((copies,)),
            pltpu.SemaphoreType.DMA((copies,)),
            pltpu.SemaphoreType.DMA((2,)),
            pltpu.VMEM((ROWS, RANK), F32),
            pltpu.VMEM((2, LEN, DIM), BF16),
            pltpu.VMEM((64, 128), F32),
            pltpu.VMEM(piece, F32),
            pltpu.VMEM((ROWS, RANK), BF16),
            pltpu.VMEM((ROWS, COLS), BF16),
            pltpu.VMEM((ROWS, RANK), F32),
            pltpu.VMEM((PIECES, COLS, WIDE), BF16),
            pltpu.VMEM((PIECES, 3, 64, WIDE), BF16),
            pltpu.VMEM((PIECES, 3, 48, WIDE), BF16),
            pltpu.VMEM((PIECES, 64, WIDE), BF16),
            pltpu.VMEM((PIECES, 48, WIDE), BF16),
            pltpu.VMEM((PIECES, COLS, WIDE), BF16),
        ]
        + COL_SCRATCH
        + COL_SCRATCH
        + [
            pltpu.VMEM((3,) + piece, F32),
            pltpu.VMEM(piece, F32),
            pltpu.VMEM(piece, F32),
            pltpu.VMEM(piece, F32),
            pltpu.VMEM((3,) + piece, F32),
            pltpu.VMEM(piece, F32),
            pltpu.VMEM((7,) + piece, F32),
            pltpu.VMEM((8, 128), F32),
            pltpu.VMEM((3, 8, 128), F32),
        ],
        compiler_params=params(0, 36),
        name="chain",
    )(sketch, acts, grads, lens, weight)


def ring_scratch(copies, front, back, width, dtype):
    return [
        pltpu.SemaphoreType.DMA((copies,)),
        pltpu.SemaphoreType.DMA((copies,)),
        pltpu.VMEM((3, front, width), dtype),
        pltpu.VMEM((3, back, width), dtype),
        pltpu.VMEM((front, width), dtype),
        pltpu.VMEM((back, width), dtype),
    ]


def row_ring(net, chunk, front):
    row, col, _, _, _ = place()
    up, down = (lax.rem(row + 1, 4), col), (lax.rem(row + 3, 4), col)
    return Ring(net, row, up, down, chunk, front), [up, down]


def unit_inverse(block):
    size, group = 128, 8
    count = size // group
    lanes = lax.broadcasted_iota(jnp.int32, (group, size), 1)
    sub = lax.broadcasted_iota(jnp.int32, (group, size), 0)

    def full(x):
        return jnp.broadcast_to(x, (group, size))

    s = [block[group * a : group * a + group] for a in range(count)]
    t = [(lanes == sub + group * a).astype(F32) for a in range(count)]
    for a in range(count):
        lo = a * group
        splat = [[full(s[b][:, lo + m : lo + m + 1]) for b in range(a, count)] for m in range(group)]
        d = [[full(splat[m][0][q : q + 1]) for m in range(group)] for q in range(group)]
        row_s = [full(s[a][q : q + 1]) for q in range(group)]
        row_t = [full(t[a][q : q + 1]) for q in range(group)]
        inv = []
        for m in range(group):
            inv.append(1.0 / d[m][m])
            for q in range(m + 1, group):
                f = d[q][m] * inv[m]
                for w in range(m + 1, group):
                    d[q][w] = d[q][w] - f * d[m][w]
                row_s[q] = row_s[q] - f * row_s[m]
                row_t[q] = row_t[q] - f * row_t[m]
        out = t[a]
        for m in range(group):
            out = jnp.where(sub == m, row_t[m] * jnp.sqrt(inv[m]), out)
        t[a] = out
        for m in reversed(range(group)):
            for q in range(m + 1, group):
                row_s[m] = row_s[m] - d[m][q] * row_s[q]
                row_t[m] = row_t[m] - d[m][q] * row_t[q]
            row_s[m] = row_s[m] * inv[m]
            row_t[m] = row_t[m] * inv[m]
        for b in range(a + 1, count):
            for m in range(group):
                s[b] = s[b] - splat[m][b - a] * row_s[m]
                t[b] = t[b] - splat[m][b - a] * row_t[m]
    return jnp.concatenate(t, axis=0)


def dot(a, b, dims, precision=None):
    return lax.dot_general(a, b, (dims, ((), ())), precision=precision, preferred_element_type=F32)


def tail_kernel(
    y_ref, scaled_ref, basis_ref, coef_ref, send_sems, recv_sems, got_f, got_b, sum_f, sum_b, own, g_ref, x_ref, m_ref, part, got, whole
):
    exact = lax.Precision.HIGHEST
    net = Net(send_sems, recv_sems)
    row, col, core, z, y = place()
    partner = (row, (y * 8 + z) * 2 + 1 - core)
    ring, peers = row_ring(net, 64, 32)
    far = (lax.rem(row + 2, 4), col)
    half = core * 256
    left = y_ref[:, pl.ds(pl.multiple_of(half, 128), 256)]
    arrived = greet(peers + [far, partner])
    own[...] = dot(left, y_ref[...], ((0,), (0,)))
    arrived()
    src = functools.partial(at_rows, own, step=8)

    def dst(start, count):
        return at_rows(g_ref, half + start, count, 8)

    ring.reduce_start(src, got_f, got_b)
    part[...] = dot(scaled_ref[...], y_ref[...], ((1,), (0,)))
    ring.reduce_relay(src, got_f, got_b, sum_f, sum_b)
    top, low = ring.reduce_end(src, got_f, got_b)
    dst(ring.own, 32)[...] = top
    dst(ring.own + 32, 32)[...] = low
    ring.gather_start(dst)
    swaps = [net.send(dst(ring.own, 64), dst(ring.own, 64), partner)]
    ring.gather_relay(dst)
    for start in (ring.last, ring.next):
        swaps.append(net.send(dst(start, 64), dst(start, 64), partner))
    ring.gather_end()
    swaps.append(net.send(dst(ring.far, 64), dst(ring.far, 64), partner))

    chunk = COLS // 4
    xpeer = [peers[0], far, peers[1]]
    for d in range(3):
        net.send(at_rows(part, lax.rem(row + d + 1, 4) * chunk, chunk), got.at[d], xpeer[d])
    scatter = net.copies[-3:]
    mine, summed = at_rows(part, row * chunk, chunk), at_rows(whole, row * chunk, chunk)
    gather = [net.make(summed, summed, peer) for peer in xpeer]
    for copy in swaps:
        copy.wait_recv()
    x_ref[...] = g_ref[...]

    size = 128
    eye = lax.broadcasted_iota(jnp.int32, (size, size), 0) == lax.broadcasted_iota(jnp.int32, (size, size), 1)

    def block(k, carry):
        at = pl.ds(pl.multiple_of(k * size, size), size)
        unit = unit_inverse(x_ref[at, at])
        x_ref[:, at] = jnp.zeros((RANK, size), F32)
        x_ref[at, at] = eye.astype(F32)
        line = dot(unit, x_ref[at, :], ((1,), (0,)), exact)
        later = lax.broadcasted_iota(jnp.int32, (size, RANK), 1) >= (k + 1) * size
        m_ref[at, :] = jnp.where(later, 0.0, line)
        x_ref[...] = x_ref[...] - dot(jnp.where(later, line, 0.0), line, ((0,), (0,)), exact)

        @pl.when(k == 1)
        def _():
            for copy in scatter:
                copy.wait_recv()
            summed[...] = mine[...] + got[0] + got[1] + got[2]
            for copy in gather:
                copy.start()

        return carry

    lax.fori_loop(0, RANK // size, block, 0)
    rows = y_ref[pl.ds(pl.multiple_of(col * 32, 16), 32)].astype(F32)
    basis_ref[...] = dot(rows, m_ref[...], ((1,), (1,)), exact) * math.sqrt(DIM)
    for copy in gather:
        copy.wait_recv()
    mine_rows = m_ref[pl.ds(pl.multiple_of(row * 128, 128), 128)]
    coef_ref[...] = dot(whole[...], mine_rows, ((1,), (1,)), exact) * math.sqrt(FF)
    net.drain()


def outputs(second, scaled):
    return pl.pallas_call(
        tail_kernel,
        out_shape=(jax.ShapeDtypeStruct((32, RANK), F32), jax.ShapeDtypeStruct((COLS, RANK // 4), F32)),
        in_specs=[VMEM, VMEM],
        out_specs=(VMEM, VMEM),
        scratch_shapes=ring_scratch(20, 32, 32, RANK, F32)
        + [
            pltpu.VMEM((256, RANK), F32),
            pltpu.VMEM((RANK, RANK), F32),
            pltpu.VMEM((RANK, RANK), F32),
            pltpu.VMEM((RANK, RANK), F32),
            pltpu.VMEM((COLS, RANK), F32),
            pltpu.VMEM((3, COLS // 4, RANK), F32),
            pltpu.VMEM((COLS, RANK), F32),
        ],
        compiler_params=params(3, 24),
        name="outputs",
    )(second, scaled)


def local(activations, out_grads, valid_len, weight, sketch):
    second, scaled = chain(sketch, activations, out_grads.transpose(0, 2, 1), valid_len, weight.T)
    basis, coeffs = outputs(second, scaled)
    return basis, coeffs.T


def solution(mesh):
    placed = (
        P("row", None, None),
        P("row", None, "col"),
        P("row"),
        P("row", "col"),
        P("col", None),
    )
    return jax.shard_map(
        local,
        mesh=mesh,
        in_specs=placed,
        out_specs=(P(("row", "col"), None), P("row", "col")),
        check_vma=False,
    )
```

```python
import functools
import math

import jax
import jax.numpy as jnp
from jax import lax
from jax.experimental import pallas as pl
from jax.experimental.pallas import tpu as pltpu
from jax.sharding import PartitionSpec as P

MESH = pl.DeviceIdType.MESH
VMEM = pl.BlockSpec(memory_space=pltpu.VMEM)
F32, BF16 = jnp.float32, jnp.bfloat16
ROWS, COLS, RANK, DIM, FF = 2048, 448, 512, 8192, 28672
HALF, YCH, ZCH, LEN = 1024, 256, 32, 256
PIECES = 4
WIDE = RANK // PIECES
ZTYPE = BF16


def f32(ref):
    return ref[...].astype(F32)


def at_rows(ref, start, count, step=16):
    return ref.at[pl.ds(pl.multiple_of(start, step), count)]


class Net:
    def __init__(self, send_sems, recv_sems):
        self.send_sems, self.recv_sems, self.copies = send_sems, recv_sems, []

    def send(self, src, dst, device):
        copy = self.make(src, dst, device)
        copy.start()
        return copy

    def make(self, src, dst, device):
        slot = len(self.copies)
        copy = pltpu.make_async_remote_copy(
            src_ref=src,
            dst_ref=dst,
            send_sem=self.send_sems.at[slot],
            recv_sem=self.recv_sems.at[slot],
            device_id=device,
            device_id_type=MESH,
        )
        self.copies.append(copy)
        return copy

    def drain(self):
        for copy in self.copies:
            copy.wait_send()


def greet(peers):
    barrier = pltpu.get_barrier_semaphore()
    for peer in peers:
        pl.semaphore_signal(barrier, inc=1, device_id=peer, device_id_type=MESH)
    return lambda: pl.semaphore_wait(barrier, len(peers))


def place():
    row, col = lax.axis_index("row"), lax.axis_index("col")
    return row, col, lax.rem(col, 2), lax.rem(col // 2, 8), col // 16


class Ring:
    def __init__(self, net, me, up, down, chunk, front):
        self.net, self.up, self.down, self.front, self.back = net, up, down, front, chunk - front
        self.own = me * chunk
        self.next = lax.rem(me + 1, 4) * chunk
        self.far = lax.rem(me + 2, 4) * chunk
        self.last = lax.rem(me + 3, 4) * chunk

    def reduce_start(self, src, got_f, got_b):
        send, front, back = self.net.send, self.front, self.back
        self.red = [
            send(src(self.far, front), got_f.at[0], self.up),
            send(src(self.far + front, back), got_b.at[0], self.down),
            send(src(self.next + front, back), got_b.at[1], self.up),
            send(src(self.last, front), got_f.at[1], self.down),
        ]

    def reduce_relay(self, src, got_f, got_b, sum_f, sum_b):
        send, front, back = self.net.send, self.front, self.back
        self.red[0].wait_recv()
        sum_f[...] = (f32(got_f.at[0]) + f32(src(self.next, front))).astype(sum_f.dtype)
        self.red.append(send(sum_f, got_f.at[2], self.up))
        self.red[1].wait_recv()
        sum_b[...] = (f32(got_b.at[0]) + f32(src(self.last + front, back))).astype(sum_b.dtype)
        self.red.append(send(sum_b, got_b.at[2], self.down))

    def reduce_end(self, src, got_f, got_b):
        for copy in self.red[2:]:
            copy.wait_recv()
        top = f32(src(self.own, self.front)) + f32(got_f.at[1]) + f32(got_f.at[2])
        low = f32(src(self.own + self.front, self.back)) + f32(got_b.at[1]) + f32(got_b.at[2])
        return top, low

    def gather_start(self, dst):
        whole = dst(self.own, self.front + self.back)
        self.gat = [self.net.send(whole, whole, self.up), self.net.send(whole, whole, self.down)]

    def gather_relay(self, dst):
        self.gat[0].wait_recv()
        part = dst(self.last, self.front)
        self.gat.append(self.net.send(part, part, self.up))
        self.gat[1].wait_recv()
        part = dst(self.next + self.front, self.back)
        self.gat.append(self.net.send(part, part, self.down))

    def gather_end(self):
        self.gat[2].wait_recv()
        self.gat[3].wait_recv()


def col_sum_steps(net, x_ref, o_ref, rescale, pair, mine, got_f, got_b, sum_f, sum_b, ysum, zgot):
    row, _, core, z, y = place()

    def at(yy, zz, kk):
        return (row, (yy * 8 + zz) * 2 + kk)

    partner = at(y, z, 1 - core)
    up, down = at(lax.rem(y + 1, 4), z, core), at(lax.rem(y + 3, 4), z, core)
    zpeer = [at(y, lax.rem(z + d, 8), core) for d in range(1, 8)]
    base, other = core * HALF, (1 - core) * HALF
    state = [dict() for _ in range(PIECES)]

    def cols(p):
        return pl.ds(p * WIDE, WIDE)

    def out(p, start, count):
        return o_ref.at[pl.ds(pl.multiple_of(base + start, 16), count), cols(p)]

    def src(p):
        return lambda start, count: mine.at[p, pl.ds(pl.multiple_of(start, 16), count)]

    def s0(p):
        half = x_ref.at[pl.ds(pl.multiple_of(other, 16), HALF), cols(p)]
        state[p]["pair"] = net.send(half, pair.at[p], partner)

    def s1(p):
        state[p]["pair"].wait_recv()
        own = x_ref.at[pl.ds(pl.multiple_of(base, 16), HALF), cols(p)]
        mine[p] = (f32(own) + f32(pair.at[p])).astype(BF16)
        ring = Ring(net, y, up, down, YCH, YCH // 2)
        state[p]["ring"] = ring
        ring.reduce_start(src(p), got_f.at[p], got_b.at[p])

    def s2(p):
        state[p]["ring"].reduce_relay(src(p), got_f.at[p], got_b.at[p], sum_f.at[p], sum_b.at[p])

    def s3(p):
        top, low = state[p]["ring"].reduce_end(src(p), got_f.at[p], got_b.at[p])
        ysum[p, pl.ds(0, YCH // 2)] = top.astype(ZTYPE)
        ysum[p, pl.ds(YCH // 2, YCH // 2)] = low.astype(ZTYPE)
        state[p]["z"] = []
        for d in range(1, 8):
            part = ysum.at[p, pl.ds(pl.multiple_of(lax.rem(z + d, 8) * ZCH, 16), ZCH)]
            state[p]["z"].append(net.send(part, zgot.at[p, d - 1], zpeer[d - 1]))

    def s4(p):
        total = f32(ysum.at[p, pl.ds(pl.multiple_of(z * ZCH, 16), ZCH)])
        for d in range(7):
            state[p]["z"][d].wait_recv()
            total = total + f32(zgot.at[p, d])
        part = out(p, y * YCH + z * ZCH, ZCH)
        part[...] = rescale(total, base + y * YCH + z * ZCH).astype(BF16)
        state[p]["g"] = [net.send(part, part, peer) for peer in zpeer]

    def s5(p):
        for copy in state[p]["g"]:
            copy.wait_recv()
        ring = state[p]["ring"]
        ring.gather_start(functools.partial(out, p))
        whole = out(p, ring.own, YCH)
        state[p]["c"] = [net.send(whole, whole, partner)]

    def s6(p):
        ring = state[p]["ring"]
        ring.gather_relay(functools.partial(out, p))
        for start in (ring.last, ring.next):
            whole = out(p, start, YCH)
            state[p]["c"].append(net.send(whole, whole, partner))

    def s7(p):
        ring = state[p]["ring"]
        ring.gather_end()
        whole = out(p, ring.far, YCH)
        state[p]["c"].append(net.send(whole, whole, partner))

    def s8(p):
        for copy in state[p]["c"]:
            copy.wait_recv()

    return [s0, s1, s2, s3, s4, s5, s6, s7, s8], [partner, up, down] + zpeer


COL_SCRATCH = [
    pltpu.VMEM((PIECES, HALF, WIDE), F32),
    pltpu.VMEM((PIECES, HALF, WIDE), BF16),
    pltpu.VMEM((PIECES, 3, YCH // 2, WIDE), BF16),
    pltpu.VMEM((PIECES, 3, YCH // 2, WIDE), BF16),
    pltpu.VMEM((PIECES, YCH // 2, WIDE), BF16),
    pltpu.VMEM((PIECES, YCH // 2, WIDE), BF16),
    pltpu.VMEM((PIECES, YCH, WIDE), ZTYPE),
    pltpu.VMEM((PIECES, 7, ZCH, WIDE), ZTYPE),
]


ORDER = (
    100, 4, 5, 101, 102, 8, 9, 6, 103, 7, 12, 13, 10, 14, 11, 104,
    105, 16, 17, 15, 110, 111, 112, 113, 18, 20, 21, 24, 19, 25, 22, 28,
    32, 36, 29, 26, 33, 37, 23, 40, 30, 44, 41, 27, 34, 38, 48, 31,
    45, 42, 35, 39, 52, 56, 46, 49, 43, 60, 50, 53, 57, 47, 64, 54,
    58, 61, 51, 68, 62, 65, 55, 59, 66, 63, 69, 70, 72, 67, 71, 73,
    74, 76, 75, 77, 78, 81, 80, 79, 82, 84, 83, 86, 85, 89, 90, 88,
    87, 91,
)


def run_steps(steps, fisher, weight):
    for event in ORDER:
        if event >= 110:
            weight[event - 110]()
        elif event >= 100:
            fisher[event - 100]()
        else:
            steps[event // PIECES](event % PIECES)


def fisher_steps(net, f_ref, scale_ref, peers, far, xpeer, fx, f1, fc, f2, fy, f3, fz, ft, fg):
    row = lax.axis_index("row")
    ypeer = [peers[1], far, peers[2]]
    state = {}

    def t0():
        state["x"] = [
            net.send(at_rows(f_ref, lax.rem(row + d, 4) * 16, 16, 8), fx.at[d - 1], xpeer[d - 1])
            for d in range(1, 4)
        ]

    def t1():
        for copy in state["x"]:
            copy.wait_recv()
        f1[...] = at_rows(f_ref, row * 16, 16, 8)[...] + fx[0] + fx[1] + fx[2]
        state["c"] = net.send(f1, fc, peers[0])

    def t2():
        state["c"].wait_recv()
        f2[...] = f1[...] + fc[...]
        state["y"] = [net.send(f2, fy.at[d], ypeer[d]) for d in range(3)]

    def t3():
        for copy in state["y"]:
            copy.wait_recv()
        f3[...] = f2[...] + fy[0] + fy[1] + fy[2]
        state["z"] = [net.send(f3, fz.at[d], peers[3 + d]) for d in range(7)]

    def t4():
        total = f3[...]
        for d in range(7):
            state["z"][d].wait_recv()
            total = total + fz[d]
        scale_ref[...] = total
        ft[...] = total[0:8] + total[8:16]
        state["t"] = [net.send(ft, fg.at[d], xpeer[d]) for d in range(3)]

    def t5():
        for copy in state["t"]:
            copy.wait_recv()
        mass = jnp.sum(ft[...] + fg[0] + fg[1] + fg[2], keepdims=True)
        scale_ref[...] = jnp.sqrt(jnp.maximum(scale_ref[...], 0.0) / (mass / DIM + 1e-06))

    return [t0, t1, t2, t3, t4, t5]


def chain_kernel(
    sketch_in, acts_ref, grads_in, len_in, weight_in, y_ref, scaled_ref, send_sems, recv_sems, load_sems, sketch_ref, grads_ref, len_ref,
    weight_ref, x_ref, acts, f_ref, scale_ref, first, back, again, part, xgot_f, xgot_b,
    xsum_f, xsum_b, projected, *scratch
):
    net = Net(send_sems, recv_sems)
    row, col, core, z, y = place()

    def rescale(total, start):
        line = scale_ref[pl.ds(start // 128, 1), :]
        lanes = lax.broadcasted_iota(jnp.int32, (ZCH, 128), 1)
        rows = lax.broadcasted_iota(jnp.int32, (ZCH, 128), 0)
        picked = jnp.where(lanes == rows + lax.rem(start, 128), line, 0.0)
        return total * jnp.sum(picked, axis=1, keepdims=True)

    sum1, peers = col_sum_steps(net, x_ref, first, rescale, *scratch[:8])
    sum2, _ = col_sum_steps(net, again, y_ref, lambda total, start: total, *scratch[8:16])
    xpeer = [(lax.rem(row + d, 4), col) for d in range(1, 4)]
    far = (row, (lax.rem(y + 2, 4) * 8 + z) * 2 + core)
    fisher = fisher_steps(net, f_ref, scale_ref, peers, far, xpeer, *scratch[16:])
    rings = [Ring(net, row, xpeer[0], xpeer[2], COLS // 4, 64) for _ in range(PIECES)]

    def scale_weight(n):
        def step():
            for b in range(4 * n, 4 * n + 4):
                at = pl.ds(b * 128, 128)
                block = weight_ref[:, at].astype(F32) * scale_ref[b : b + 1, :]
                scaled_ref[:, at] = block.astype(BF16)
                back[at, :] = block.T.astype(BF16)

        return step

    def src(p):
        return lambda start, count: at_rows(part.at[p], start, count)

    def dst(p):
        return lambda start, count: at_rows(projected.at[p], start, count)

    def q0(p):
        part[p] = dot(scaled_ref[...], first[:, pl.ds(p * WIDE, WIDE)], ((1,), (0,))).astype(BF16)
        rings[p].reduce_start(src(p), xgot_f.at[p], xgot_b.at[p])

    def q1(p):
        rings[p].reduce_relay(src(p), xgot_f.at[p], xgot_b.at[p], xsum_f.at[p], xsum_b.at[p])

    def q2(p):
        top, low = rings[p].reduce_end(src(p), xgot_f.at[p], xgot_b.at[p])
        dst(p)(rings[p].own, 64)[...] = top.astype(BF16)
        dst(p)(rings[p].own + 64, 48)[...] = low.astype(BF16)
        rings[p].gather_start(dst(p))

    def q3(p):
        rings[p].gather_relay(dst(p))

    def q4(p):
        rings[p].gather_end()
        again[:, pl.ds(p * WIDE, WIDE)] = dot(back[...], projected[p], ((1,), (0,)))

    moves = [(weight_in, weight_ref), (sketch_in, sketch_ref), (grads_in, grads_ref), (len_in, len_ref)]
    moves += [(acts_ref.at[n], acts.at[n]) for n in range(2)]
    loads = [pltpu.make_async_copy(a, b, load_sems.at[n]) for n, (a, b) in enumerate(moves)]
    for load in loads:
        load.start()
    arrived = greet(peers + [far] + xpeer)
    for load in loads[:2]:
        load.wait()
    for n in range(4):
        at = pl.ds(n * 512, 512)
        x_ref[at, :] = dot(weight_ref[:, at], sketch_ref[...], ((0,), (0,)))

    def masses(n):
        loads[4 + n].wait()
        valid = lax.broadcasted_iota(jnp.int32, (COLS, LEN), 1) < len_ref[n]
        grads = jnp.where(valid, grads_ref[n].astype(F32), 0.0).astype(BF16)
        tokens = dot(grads, grads, ((0,), (0,)))
        high = tokens.astype(BF16)
        low = (tokens - high.astype(F32)).astype(BF16)
        for c in range(8):
            block = acts[n, :, pl.ds(c * 1024, 1024)]
            mixed = dot(high, block, ((1,), (0,))) + dot(low, block, ((1,), (0,)))
            sums = jnp.sum(block.astype(F32) * mixed, axis=0, keepdims=True)
            for i in range(8):
                at = pl.ds(8 * c + i, 1)
                line = sums[:, i * 128 : (i + 1) * 128]
                f_ref[at, :] = line if n == 0 else f_ref[at, :] + line

    for load in loads[2:4]:
        load.wait()
    masses(0)
    arrived()
    for p in range(PIECES):
        sum1[0](p)
    masses(1)
    run_steps(sum1 + [q0, q1, q2, q3, q4] + sum2, fisher, [scale_weight(n) for n in range(4)])
    net.drain()


def params(collective_id, mib):
    return pltpu.CompilerParams(
        collective_id=collective_id, has_side_effects=True, vmem_limit_bytes=mib << 20
    )


def chain(sketch, acts, grads, lens, weight):
    piece = (16, 128)
    copies = PIECES * 68 + 17
    return pl.pallas_call(
        chain_kernel,
        out_shape=(jax.ShapeDtypeStruct((ROWS, RANK), BF16), jax.ShapeDtypeStruct((COLS, ROWS), BF16)),
        in_specs=[pl.BlockSpec(memory_space=pltpu.HBM)] * 5,
        out_specs=(VMEM, VMEM),
        scratch_shapes=[
            pltpu.SemaphoreType.DMA((copies,)),
            pltpu.SemaphoreType.DMA((copies,)),
            pltpu.SemaphoreType.DMA((6,)),
            pltpu.VMEM((COLS, RANK), BF16),
            pltpu.VMEM((2, COLS, LEN), BF16),
            pltpu.SMEM((2,), jnp.int32),
            pltpu.VMEM((COLS, ROWS), BF16),
            pltpu.VMEM((ROWS, RANK), F32),
            pltpu.VMEM((2, LEN, DIM), BF16),
            pltpu.VMEM((64, 128), F32),
            pltpu.VMEM(piece, F32),
            pltpu.VMEM((ROWS, RANK), BF16),
            pltpu.VMEM((ROWS, COLS), BF16),
            pltpu.VMEM((ROWS, RANK), F32),
            pltpu.VMEM((PIECES, COLS, WIDE), BF16),
            pltpu.VMEM((PIECES, 3, 64, WIDE), BF16),
            pltpu.VMEM((PIECES, 3, 48, WIDE), BF16),
            pltpu.VMEM((PIECES, 64, WIDE), BF16),
            pltpu.VMEM((PIECES, 48, WIDE), BF16),
            pltpu.VMEM((PIECES, COLS, WIDE), BF16),
        ]
        + COL_SCRATCH
        + COL_SCRATCH
        + [
            pltpu.VMEM((3,) + piece, F32),
            pltpu.VMEM(piece, F32),
            pltpu.VMEM(piece, F32),
            pltpu.VMEM(piece, F32),
            pltpu.VMEM((3,) + piece, F32),
            pltpu.VMEM(piece, F32),
            pltpu.VMEM((7,) + piece, F32),
            pltpu.VMEM((8, 128), F32),
            pltpu.VMEM((3, 8, 128), F32),
        ],
        compiler_params=params(0, 36),
        name="chain",
    )(sketch, acts, grads, lens, weight)


def ring_scratch(copies, front, back, width, dtype):
    return [
        pltpu.SemaphoreType.DMA((copies,)),
        pltpu.SemaphoreType.DMA((copies,)),
        pltpu.VMEM((3, front, width), dtype),
        pltpu.VMEM((3, back, width), dtype),
        pltpu.VMEM((front, width), dtype),
        pltpu.VMEM((back, width), dtype),
    ]


def row_ring(net, chunk, front):
    row, col, _, _, _ = place()
    up, down = (lax.rem(row + 1, 4), col), (lax.rem(row + 3, 4), col)
    return Ring(net, row, up, down, chunk, front), [up, down]


def unit_inverse(block):
    size, group = 128, 8
    count = size // group
    lanes = lax.broadcasted_iota(jnp.int32, (group, size), 1)
    sub = lax.broadcasted_iota(jnp.int32, (group, size), 0)

    def full(x):
        return jnp.broadcast_to(x, (group, size))

    s = [block[group * a : group * a + group] for a in range(count)]
    t = [(lanes == sub + group * a).astype(F32) for a in range(count)]
    for a in range(count):
        lo = a * group
        splat = [[full(s[b][:, lo + m : lo + m + 1]) for b in range(a, count)] for m in range(group)]
        d = [[full(splat[m][0][q : q + 1]) for m in range(group)] for q in range(group)]
        row_s = [full(s[a][q : q + 1]) for q in range(group)]
        row_t = [full(t[a][q : q + 1]) for q in range(group)]
        inv = []
        for m in range(group):
            inv.append(1.0 / d[m][m])
            for q in range(m + 1, group):
                f = d[q][m] * inv[m]
                for w in range(m + 1, group):
                    d[q][w] = d[q][w] - f * d[m][w]
                row_s[q] = row_s[q] - f * row_s[m]
                row_t[q] = row_t[q] - f * row_t[m]
        out = t[a]
        for m in range(group):
            out = jnp.where(sub == m, row_t[m] * jnp.sqrt(inv[m]), out)
        t[a] = out
        for m in reversed(range(group)):
            for q in range(m + 1, group):
                row_s[m] = row_s[m] - d[m][q] * row_s[q]
                row_t[m] = row_t[m] - d[m][q] * row_t[q]
            row_s[m] = row_s[m] * inv[m]
            row_t[m] = row_t[m] * inv[m]
        for b in range(a + 1, count):
            for m in range(group):
                s[b] = s[b] - splat[m][b - a] * row_s[m]
                t[b] = t[b] - splat[m][b - a] * row_t[m]
    return jnp.concatenate(t, axis=0)


def dot(a, b, dims, precision=None):
    return lax.dot_general(a, b, (dims, ((), ())), precision=precision, preferred_element_type=F32)


def tail_kernel(
    y_ref, scaled_ref, basis_ref, coef_ref, send_sems, recv_sems, got_f, got_b, sum_f, sum_b, own, g_ref, x_ref, m_ref, part, got, whole
):
    exact = lax.Precision.HIGHEST
    net = Net(send_sems, recv_sems)
    row, col, core, z, y = place()
    partner = (row, (y * 8 + z) * 2 + 1 - core)
    ring, peers = row_ring(net, 64, 32)
    far = (lax.rem(row + 2, 4), col)
    half = core * 256
    left = y_ref[:, pl.ds(pl.multiple_of(half, 128), 256)]
    arrived = greet(peers + [far, partner])
    own[...] = dot(left, y_ref[...], ((0,), (0,)))
    arrived()
    src = functools.partial(at_rows, own, step=8)

    def dst(start, count):
        return at_rows(g_ref, half + start, count, 8)

    ring.reduce_start(src, got_f, got_b)
    part[...] = dot(scaled_ref[...], y_ref[...], ((1,), (0,)))
    ring.reduce_relay(src, got_f, got_b, sum_f, sum_b)
    top, low = ring.reduce_end(src, got_f, got_b)
    dst(ring.own, 32)[...] = top
    dst(ring.own + 32, 32)[...] = low
    ring.gather_start(dst)
    swaps = [net.send(dst(ring.own, 64), dst(ring.own, 64), partner)]
    ring.gather_relay(dst)
    for start in (ring.last, ring.next):
        swaps.append(net.send(dst(start, 64), dst(start, 64), partner))
    ring.gather_end()
    swaps.append(net.send(dst(ring.far, 64), dst(ring.far, 64), partner))

    chunk = COLS // 4
    xpeer = [peers[0], far, peers[1]]
    for d in range(3):
        net.send(at_rows(part, lax.rem(row + d + 1, 4) * chunk, chunk), got.at[d], xpeer[d])
    scatter = net.copies[-3:]
    mine, summed = at_rows(part, row * chunk, chunk), at_rows(whole, row * chunk, chunk)
    gather = [net.make(summed, summed, peer) for peer in xpeer]
    for copy in swaps:
        copy.wait_recv()
    x_ref[...] = g_ref[...]

    size = 128
    eye = lax.broadcasted_iota(jnp.int32, (size, size), 0) == lax.broadcasted_iota(jnp.int32, (size, size), 1)

    def block(k, carry):
        at = pl.ds(pl.multiple_of(k * size, size), size)
        unit = unit_inverse(x_ref[at, at])
        x_ref[:, at] = jnp.zeros((RANK, size), F32)
        x_ref[at, at] = eye.astype(F32)
        line = dot(unit, x_ref[at, :], ((1,), (0,)), exact)
        later = lax.broadcasted_iota(jnp.int32, (size, RANK), 1) >= (k + 1) * size
        m_ref[at, :] = jnp.where(later, 0.0, line)
        x_ref[...] = x_ref[...] - dot(jnp.where(later, line, 0.0), line, ((0,), (0,)), exact)

        @pl.when(k == 1)
        def _():
            for copy in scatter:
                copy.wait_recv()
            summed[...] = mine[...] + got[0] + got[1] + got[2]
            for copy in gather:
                copy.start()

        return carry

    lax.fori_loop(0, RANK // size, block, 0)
    rows = y_ref[pl.ds(pl.multiple_of(col * 32, 16), 32)].astype(F32)
    basis_ref[...] = dot(rows, m_ref[...], ((1,), (1,)), exact) * math.sqrt(DIM)
    for copy in gather:
        copy.wait_recv()
    mine_rows = m_ref[pl.ds(pl.multiple_of(row * 128, 128), 128)]
    coef_ref[...] = dot(whole[...], mine_rows, ((1,), (1,)), exact) * math.sqrt(FF)
    net.drain()


def outputs(second, scaled):
    return pl.pallas_call(
        tail_kernel,
        out_shape=(jax.ShapeDtypeStruct((32, RANK), F32), jax.ShapeDtypeStruct((COLS, RANK // 4), F32)),
        in_specs=[VMEM, VMEM],
        out_specs=(VMEM, VMEM),
        scratch_shapes=ring_scratch(20, 32, 32, RANK, F32)
        + [
            pltpu.VMEM((256, RANK), F32),
            pltpu.VMEM((RANK, RANK), F32),
            pltpu.VMEM((RANK, RANK), F32),
            pltpu.VMEM((RANK, RANK), F32),
            pltpu.VMEM((COLS, RANK), F32),
            pltpu.VMEM((3, COLS // 4, RANK), F32),
            pltpu.VMEM((COLS, RANK), F32),
        ],
        compiler_params=params(3, 24),
        name="outputs",
    )(second, scaled)


def local(activations, out_grads, valid_len, weight, sketch):
    arrays = (sketch, activations, out_grads.transpose(0, 2, 1), valid_len, weight.T)
    second, scaled = chain(*(pltpu.with_memory_space_constraint(a, pltpu.HBM) for a in arrays))
    basis, coeffs = outputs(second, scaled)
    return basis, coeffs.T


def solution(mesh):
    placed = (
        P("row", None, None),
        P("row", None, "col"),
        P("row"),
        P("row", "col"),
        P("col", None),
    )
    return jax.shard_map(
        local,
        mesh=mesh,
        in_specs=placed,
        out_specs=(P(("row", "col"), None), P("row", "col")),
        check_vma=False,
    )
```

```python
import functools
import math

import jax
import jax.numpy as jnp
from jax import lax
from jax.experimental import pallas as pl
from jax.experimental.pallas import tpu as pltpu
from jax.sharding import PartitionSpec as P

MESH = pl.DeviceIdType.MESH
VMEM = pl.BlockSpec(memory_space=pltpu.VMEM)
F32, BF16 = jnp.float32, jnp.bfloat16
ROWS, COLS, RANK, DIM, FF = 2048, 448, 512, 8192, 28672
HALF, YCH, ZCH, LEN = 1024, 256, 32, 256
PIECES = 4
WIDE = RANK // PIECES
ZTYPE = BF16


def f32(ref):
    return ref[...].astype(F32)


def at_rows(ref, start, count, step=16):
    return ref.at[pl.ds(pl.multiple_of(start, step), count)]


class Net:
    def __init__(self, send_sems, recv_sems):
        self.send_sems, self.recv_sems, self.copies = send_sems, recv_sems, []

    def send(self, src, dst, device):
        copy = self.make(src, dst, device)
        copy.start()
        return copy

    def make(self, src, dst, device):
        slot = len(self.copies)
        copy = pltpu.make_async_remote_copy(
            src_ref=src,
            dst_ref=dst,
            send_sem=self.send_sems.at[slot],
            recv_sem=self.recv_sems.at[slot],
            device_id=device,
            device_id_type=MESH,
        )
        self.copies.append(copy)
        return copy

    def drain(self):
        for copy in self.copies:
            copy.wait_send()


def greet(peers):
    barrier = pltpu.get_barrier_semaphore()
    for peer in peers:
        pl.semaphore_signal(barrier, inc=1, device_id=peer, device_id_type=MESH)
    return lambda: pl.semaphore_wait(barrier, len(peers))


def place():
    row, col = lax.axis_index("row"), lax.axis_index("col")
    return row, col, lax.rem(col, 2), lax.rem(col // 2, 8), col // 16


class Ring:
    def __init__(self, net, me, up, down, chunk, front):
        self.net, self.up, self.down, self.front, self.back = net, up, down, front, chunk - front
        self.own = me * chunk
        self.next = lax.rem(me + 1, 4) * chunk
        self.far = lax.rem(me + 2, 4) * chunk
        self.last = lax.rem(me + 3, 4) * chunk

    def reduce_start(self, src, got_f, got_b):
        send, front, back = self.net.send, self.front, self.back
        self.red = [
            send(src(self.far, front), got_f.at[0], self.up),
            send(src(self.far + front, back), got_b.at[0], self.down),
            send(src(self.next + front, back), got_b.at[1], self.up),
            send(src(self.last, front), got_f.at[1], self.down),
        ]

    def reduce_relay(self, src, got_f, got_b, sum_f, sum_b):
        send, front, back = self.net.send, self.front, self.back
        self.red[0].wait_recv()
        sum_f[...] = (f32(got_f.at[0]) + f32(src(self.next, front))).astype(sum_f.dtype)
        self.red.append(send(sum_f, got_f.at[2], self.up))
        self.red[1].wait_recv()
        sum_b[...] = (f32(got_b.at[0]) + f32(src(self.last + front, back))).astype(sum_b.dtype)
        self.red.append(send(sum_b, got_b.at[2], self.down))

    def reduce_end(self, src, got_f, got_b):
        for copy in self.red[2:]:
            copy.wait_recv()
        top = f32(src(self.own, self.front)) + f32(got_f.at[1]) + f32(got_f.at[2])
        low = f32(src(self.own + self.front, self.back)) + f32(got_b.at[1]) + f32(got_b.at[2])
        return top, low

    def gather_start(self, dst):
        whole = dst(self.own, self.front + self.back)
        self.gat = [self.net.send(whole, whole, self.up), self.net.send(whole, whole, self.down)]

    def gather_relay(self, dst):
        self.gat[0].wait_recv()
        part = dst(self.last, self.front)
        self.gat.append(self.net.send(part, part, self.up))
        self.gat[1].wait_recv()
        part = dst(self.next + self.front, self.back)
        self.gat.append(self.net.send(part, part, self.down))

    def gather_end(self):
        self.gat[2].wait_recv()
        self.gat[3].wait_recv()


def col_sum_steps(net, x_ref, o_ref, rescale, pair, mine, got_f, got_b, sum_f, sum_b, ysum, zgot):
    row, _, core, z, y = place()

    def at(yy, zz, kk):
        return (row, (yy * 8 + zz) * 2 + kk)

    partner = at(y, z, 1 - core)
    up, down = at(lax.rem(y + 1, 4), z, core), at(lax.rem(y + 3, 4), z, core)
    zpeer = [at(y, lax.rem(z + d, 8), core) for d in range(1, 8)]
    base, other = core * HALF, (1 - core) * HALF
    state = [dict() for _ in range(PIECES)]

    def cols(p):
        return pl.ds(p * WIDE, WIDE)

    def out(p, start, count):
        return o_ref.at[pl.ds(pl.multiple_of(base + start, 16), count), cols(p)]

    def src(p):
        return lambda start, count: mine.at[p, pl.ds(pl.multiple_of(start, 16), count)]

    def s0(p):
        half = x_ref.at[pl.ds(pl.multiple_of(other, 16), HALF), cols(p)]
        state[p]["pair"] = net.send(half, pair.at[p], partner)

    def s1(p):
        state[p]["pair"].wait_recv()
        own = x_ref.at[pl.ds(pl.multiple_of(base, 16), HALF), cols(p)]
        mine[p] = (f32(own) + f32(pair.at[p])).astype(BF16)
        ring = Ring(net, y, up, down, YCH, YCH // 2)
        state[p]["ring"] = ring
        ring.reduce_start(src(p), got_f.at[p], got_b.at[p])

    def s2(p):
        state[p]["ring"].reduce_relay(src(p), got_f.at[p], got_b.at[p], sum_f.at[p], sum_b.at[p])

    def s3(p):
        top, low = state[p]["ring"].reduce_end(src(p), got_f.at[p], got_b.at[p])
        ysum[p, pl.ds(0, YCH // 2)] = top.astype(ZTYPE)
        ysum[p, pl.ds(YCH // 2, YCH // 2)] = low.astype(ZTYPE)
        state[p]["z"] = []
        for d in range(1, 8):
            part = ysum.at[p, pl.ds(pl.multiple_of(lax.rem(z + d, 8) * ZCH, 16), ZCH)]
            state[p]["z"].append(net.send(part, zgot.at[p, d - 1], zpeer[d - 1]))

    def s4(p):
        total = f32(ysum.at[p, pl.ds(pl.multiple_of(z * ZCH, 16), ZCH)])
        for d in range(7):
            state[p]["z"][d].wait_recv()
            total = total + f32(zgot.at[p, d])
        part = out(p, y * YCH + z * ZCH, ZCH)
        part[...] = rescale(total, base + y * YCH + z * ZCH).astype(BF16)
        state[p]["g"] = [net.send(part, part, peer) for peer in zpeer]

    def s5(p):
        for copy in state[p]["g"]:
            copy.wait_recv()
        ring = state[p]["ring"]
        ring.gather_start(functools.partial(out, p))
        whole = out(p, ring.own, YCH)
        state[p]["c"] = [net.send(whole, whole, partner)]

    def s6(p):
        ring = state[p]["ring"]
        ring.gather_relay(functools.partial(out, p))
        for start in (ring.last, ring.next):
            whole = out(p, start, YCH)
            state[p]["c"].append(net.send(whole, whole, partner))

    def s7(p):
        ring = state[p]["ring"]
        ring.gather_end()
        whole = out(p, ring.far, YCH)
        state[p]["c"].append(net.send(whole, whole, partner))

    def s8(p):
        for copy in state[p]["c"]:
            copy.wait_recv()

    return [s0, s1, s2, s3, s4, s5, s6, s7, s8], [partner, up, down] + zpeer


COL_SCRATCH = [
    pltpu.VMEM((PIECES, HALF, WIDE), F32),
    pltpu.VMEM((PIECES, HALF, WIDE), BF16),
    pltpu.VMEM((PIECES, 3, YCH // 2, WIDE), BF16),
    pltpu.VMEM((PIECES, 3, YCH // 2, WIDE), BF16),
    pltpu.VMEM((PIECES, YCH // 2, WIDE), BF16),
    pltpu.VMEM((PIECES, YCH // 2, WIDE), BF16),
    pltpu.VMEM((PIECES, YCH, WIDE), ZTYPE),
    pltpu.VMEM((PIECES, 7, ZCH, WIDE), ZTYPE),
]


ORDER = (
    100, 4, 5, 101, 102, 8, 9, 6, 103, 7, 12, 13, 10, 14, 11, 104,
    105, 16, 17, 15, 110, 111, 112, 113, 18, 20, 21, 24, 19, 25, 22, 28,
    32, 36, 29, 26, 33, 37, 23, 40, 30, 44, 41, 27, 34, 38, 48, 31,
    45, 42, 35, 39, 52, 56, 46, 49, 43, 60, 50, 53, 57, 47, 64, 54,
    58, 61, 51, 68, 62, 65, 55, 59, 66, 63, 69, 70, 72, 67, 71, 73,
    74, 76, 75, 77, 78, 81, 80, 79, 82, 84, 83, 86, 85, 89, 90, 88,
    87, 91,
)


def run_steps(steps, fisher, weight):
    for event in ORDER:
        if event >= 110:
            weight[event - 110]()
        elif event >= 100:
            fisher[event - 100]()
        else:
            steps[event // PIECES](event % PIECES)


def fisher_steps(net, f_ref, scale_ref, peers, far, xpeer, fx, f1, fc, f2, fy, f3, fz, ft, fg):
    row = lax.axis_index("row")
    ypeer = [peers[1], far, peers[2]]
    state = {}

    def t0():
        state["x"] = [
            net.send(at_rows(f_ref, lax.rem(row + d, 4) * 16, 16, 8), fx.at[d - 1], xpeer[d - 1])
            for d in range(1, 4)
        ]

    def t1():
        for copy in state["x"]:
            copy.wait_recv()
        f1[...] = at_rows(f_ref, row * 16, 16, 8)[...] + fx[0] + fx[1] + fx[2]
        state["c"] = net.send(f1, fc, peers[0])

    def t2():
        state["c"].wait_recv()
        f2[...] = f1[...] + fc[...]
        state["y"] = [net.send(f2, fy.at[d], ypeer[d]) for d in range(3)]

    def t3():
        for copy in state["y"]:
            copy.wait_recv()
        f3[...] = f2[...] + fy[0] + fy[1] + fy[2]
        state["z"] = [net.send(f3, fz.at[d], peers[3 + d]) for d in range(7)]

    def t4():
        total = f3[...]
        for d in range(7):
            state["z"][d].wait_recv()
            total = total + fz[d]
        scale_ref[...] = total
        ft[...] = total[0:8] + total[8:16]
        state["t"] = [net.send(ft, fg.at[d], xpeer[d]) for d in range(3)]

    def t5():
        for copy in state["t"]:
            copy.wait_recv()
        mass = jnp.sum(ft[...] + fg[0] + fg[1] + fg[2], keepdims=True)
        scale_ref[...] = jnp.sqrt(jnp.maximum(scale_ref[...], 0.0) / (mass / DIM + 1e-06))

    return [t0, t1, t2, t3, t4, t5]


def chain_kernel(
    sketch_in, acts_ref, grads_in, len_in, weight_in, y_ref, scaled_ref, send_sems, recv_sems, load_sems, sketch_ref, grads_ref, len_ref,
    weight_ref, x_ref, acts, f_ref, scale_ref, first, back, again, part, xgot_f, xgot_b,
    xsum_f, xsum_b, projected, *scratch
):
    net = Net(send_sems, recv_sems)
    row, col, core, z, y = place()

    def rescale(total, start):
        line = scale_ref[pl.ds(start // 128, 1), :]
        lanes = lax.broadcasted_iota(jnp.int32, (ZCH, 128), 1)
        rows = lax.broadcasted_iota(jnp.int32, (ZCH, 128), 0)
        picked = jnp.where(lanes == rows + lax.rem(start, 128), line, 0.0)
        return total * jnp.sum(picked, axis=1, keepdims=True)

    sum1, peers = col_sum_steps(net, x_ref, first, rescale, *scratch[:8])
    sum2, _ = col_sum_steps(net, again, y_ref, lambda total, start: total, *scratch[8:16])
    xpeer = [(lax.rem(row + d, 4), col) for d in range(1, 4)]
    far = (row, (lax.rem(y + 2, 4) * 8 + z) * 2 + core)
    fisher = fisher_steps(net, f_ref, scale_ref, peers, far, xpeer, *scratch[16:])
    rings = [Ring(net, row, xpeer[0], xpeer[2], COLS // 4, 64) for _ in range(PIECES)]

    def scale_weight(n):
        def step():
            for b in range(4 * n, 4 * n + 4):
                at = pl.ds(b * 128, 128)
                block = weight_ref[:, at].astype(F32) * scale_ref[b : b + 1, :]
                scaled_ref[:, at] = block.astype(BF16)
                back[at, :] = block.T.astype(BF16)

        return step

    def src(p):
        return lambda start, count: at_rows(part.at[p], start, count)

    def dst(p):
        return lambda start, count: at_rows(projected.at[p], start, count)

    def q0(p):
        part[p] = dot(scaled_ref[...], first[:, pl.ds(p * WIDE, WIDE)], ((1,), (0,))).astype(BF16)
        rings[p].reduce_start(src(p), xgot_f.at[p], xgot_b.at[p])

    def q1(p):
        rings[p].reduce_relay(src(p), xgot_f.at[p], xgot_b.at[p], xsum_f.at[p], xsum_b.at[p])

    def q2(p):
        top, low = rings[p].reduce_end(src(p), xgot_f.at[p], xgot_b.at[p])
        dst(p)(rings[p].own, 64)[...] = top.astype(BF16)
        dst(p)(rings[p].own + 64, 48)[...] = low.astype(BF16)
        rings[p].gather_start(dst(p))

    def q3(p):
        rings[p].gather_relay(dst(p))

    def q4(p):
        rings[p].gather_end()
        again[:, pl.ds(p * WIDE, WIDE)] = dot(back[...], projected[p], ((1,), (0,)))

    moves = [(weight_in, weight_ref), (sketch_in, sketch_ref), (grads_in, grads_ref), (len_in, len_ref)]
    moves += [(acts_ref.at[n], acts.at[n]) for n in range(2)]
    loads = [pltpu.make_async_copy(a, b, load_sems.at[n]) for n, (a, b) in enumerate(moves)]
    for load in loads:
        load.start()
    arrived = greet(peers + [far] + xpeer)
    for load in loads[:2]:
        load.wait()
    for n in range(4):
        at = pl.ds(n * 512, 512)
        x_ref[at, :] = dot(weight_ref[:, at], sketch_ref[...], ((0,), (0,)))

    def masses(n):
        loads[4 + n].wait()
        valid = lax.broadcasted_iota(jnp.int32, (COLS, LEN), 1) < len_ref[n]
        grads = jnp.where(valid, grads_ref[n].astype(F32), 0.0).astype(BF16)
        tokens = dot(grads, grads, ((0,), (0,)))
        high = tokens.astype(BF16)
        low = (tokens - high.astype(F32)).astype(BF16)
        for c in range(8):
            block = acts[n, :, pl.ds(c * 1024, 1024)]
            mixed = dot(high, block, ((1,), (0,))) + dot(low, block, ((1,), (0,)))
            sums = jnp.sum(block.astype(F32) * mixed, axis=0, keepdims=True)
            for i in range(8):
                at = pl.ds(8 * c + i, 1)
                line = sums[:, i * 128 : (i + 1) * 128]
                f_ref[at, :] = line if n == 0 else f_ref[at, :] + line

    for load in loads[2:4]:
        load.wait()
    masses(0)
    arrived()
    for p in range(PIECES):
        sum1[0](p)
    masses(1)
    run_steps(sum1 + [q0, q1, q2, q3, q4] + sum2, fisher, [scale_weight(n) for n in range(4)])
    net.drain()


def params(collective_id, mib):
    return pltpu.CompilerParams(
        collective_id=collective_id, has_side_effects=True, vmem_limit_bytes=mib << 20
    )


def chain(sketch, acts, grads, lens, weight):
    piece = (16, 128)
    copies = PIECES * 68 + 17
    return pl.pallas_call(
        chain_kernel,
        out_shape=(jax.ShapeDtypeStruct((ROWS, RANK), BF16), jax.ShapeDtypeStruct((COLS, ROWS), BF16)),
        in_specs=[pl.BlockSpec(memory_space=pltpu.HBM)] * 5,
        out_specs=(VMEM, VMEM),
        scratch_shapes=[
            pltpu.SemaphoreType.DMA((copies,)),
            pltpu.SemaphoreType.DMA((copies,)),
            pltpu.SemaphoreType.DMA((6,)),
            pltpu.VMEM((COLS, RANK), BF16),
            pltpu.VMEM((2, COLS, LEN), BF16),
            pltpu.SMEM((2,), jnp.int32),
            pltpu.VMEM((COLS, ROWS), BF16),
            pltpu.VMEM((ROWS, RANK), F32),
            pltpu.VMEM((2, LEN, DIM), BF16),
            pltpu.VMEM((64, 128), F32),
            pltpu.VMEM(piece, F32),
            pltpu.VMEM((ROWS, RANK), BF16),
            pltpu.VMEM((ROWS, COLS), BF16),
            pltpu.VMEM((ROWS, RANK), F32),
            pltpu.VMEM((PIECES, COLS, WIDE), BF16),
            pltpu.VMEM((PIECES, 3, 64, WIDE), BF16),
            pltpu.VMEM((PIECES, 3, 48, WIDE), BF16),
            pltpu.VMEM((PIECES, 64, WIDE), BF16),
            pltpu.VMEM((PIECES, 48, WIDE), BF16),
            pltpu.VMEM((PIECES, COLS, WIDE), BF16),
        ]
        + COL_SCRATCH
        + COL_SCRATCH
        + [
            pltpu.VMEM((3,) + piece, F32),
            pltpu.VMEM(piece, F32),
            pltpu.VMEM(piece, F32),
            pltpu.VMEM(piece, F32),
            pltpu.VMEM((3,) + piece, F32),
            pltpu.VMEM(piece, F32),
            pltpu.VMEM((7,) + piece, F32),
            pltpu.VMEM((8, 128), F32),
            pltpu.VMEM((3, 8, 128), F32),
        ],
        compiler_params=params(0, 36),
        name="chain",
    )(sketch, acts, grads, lens, weight)


def exchange_scratch(rows, width, half):
    return [pltpu.VMEM((rows, width), F32)] * 2 + [
        pltpu.VMEM((3, half, width), F32),
        pltpu.VMEM((3, half, width), F32),
        pltpu.VMEM((half, width), F32),
        pltpu.VMEM((half, width), F32),
    ]


def unit_inverse(block):
    size, group = 128, 8
    count = size // group
    lanes = lax.broadcasted_iota(jnp.int32, (group, size), 1)
    sub = lax.broadcasted_iota(jnp.int32, (group, size), 0)

    def full(x):
        return jnp.broadcast_to(x, (group, size))

    s = [block[group * a : group * a + group] for a in range(count)]
    t = [(lanes == sub + group * a).astype(F32) for a in range(count)]
    for a in range(count):
        lo = a * group
        splat = [[full(s[b][:, lo + m : lo + m + 1]) for b in range(a, count)] for m in range(group)]
        d = [[full(splat[m][0][q : q + 1]) for m in range(group)] for q in range(group)]
        row_s = [full(s[a][q : q + 1]) for q in range(group)]
        row_t = [full(t[a][q : q + 1]) for q in range(group)]
        inv = []
        for m in range(group):
            inv.append(1.0 / d[m][m])
            for q in range(m + 1, group):
                f = d[q][m] * inv[m]
                for w in range(m + 1, group):
                    d[q][w] = d[q][w] - f * d[m][w]
                row_s[q] = row_s[q] - f * row_s[m]
                row_t[q] = row_t[q] - f * row_t[m]
        out = t[a]
        for m in range(group):
            out = jnp.where(sub == m, row_t[m] * jnp.sqrt(inv[m]), out)
        t[a] = out
        for m in reversed(range(group)):
            for q in range(m + 1, group):
                row_s[m] = row_s[m] - d[m][q] * row_s[q]
                row_t[m] = row_t[m] - d[m][q] * row_t[q]
            row_s[m] = row_s[m] * inv[m]
            row_t[m] = row_t[m] * inv[m]
        for b in range(a + 1, count):
            for m in range(group):
                s[b] = s[b] - splat[m][b - a] * row_s[m]
                t[b] = t[b] - splat[m][b - a] * row_t[m]
    return jnp.concatenate(t, axis=0)


def dot(a, b, dims, precision=None):
    return lax.dot_general(a, b, (dims, ((), ())), precision=precision, preferred_element_type=F32)


def tail_kernel(
    y_ref, scaled_ref, basis_ref, coef_ref, send_sems, recv_sems, x_ref, m_ref, part, got, whole, *scratch
):
    exact = lax.Precision.HIGHEST
    net = Net(send_sems, recv_sems)
    row, col, core, z, y = place()
    partner = (row, (y * 8 + z) * 2 + 1 - core)
    up, down, far = [(lax.rem(row + d, 4), col) for d in (1, 3, 2)]
    arrived = greet([up, down, far, partner])

    def exchange(width, first, chunk, own, total, got_f, got_b, sum_f, sum_b):
        ring, swaps = Ring(net, row, up, down, chunk, chunk // 2), []
        base = core * 4 * chunk

        def src(start, count):
            return at_rows(own, base + start, count, 8)

        def dst(start, count):
            return at_rows(total, base + start, count, 8)

        def swap(start):
            swaps.append(net.send(dst(start, chunk), dst(start, chunk), partner))

        def product():
            side = y_ref[:, first : first + width]
            own[...] = dot(side, y_ref[:, first:], ((0,), (0,)))

        def middle():
            top, low = ring.reduce_end(src, got_f, got_b)
            dst(ring.own, chunk // 2)[...] = top
            dst(ring.own + chunk // 2, chunk // 2)[...] = low
            ring.gather_start(dst)
            swap(ring.own)

        def relay():
            ring.gather_relay(dst)
            swap(ring.last)
            swap(ring.next)

        def end():
            ring.gather_end()
            swap(ring.far)

        def wait():
            for copy in swaps:
                copy.wait_recv()

        start = functools.partial(ring.reduce_start, src, got_f, got_b)
        turn = functools.partial(ring.reduce_relay, src, got_f, got_b, sum_f, sum_b)
        return product, start, turn, middle, relay, end, wait

    one = exchange(128, 0, 16, *scratch[:6])
    two = exchange(384, 128, 48, *scratch[6:])
    one[0]()
    arrived()
    one[1]()
    two[0]()
    two[1]()
    one[2]()
    part[...] = dot(scaled_ref[...], y_ref[...], ((1,), (0,)))
    for stage in (3, 4):
        one[stage]()
        two[stage - 1]()
    one[5]()
    two[4]()
    two[5]()

    chunk = COLS // 4
    xpeer = [up, far, down]
    for d in range(3):
        net.send(at_rows(part, lax.rem(row + d + 1, 4) * chunk, chunk), got.at[d], xpeer[d])
    scatter = net.copies[-3:]
    mine, summed = at_rows(part, row * chunk, chunk), at_rows(whole, row * chunk, chunk)
    gather = [net.make(summed, summed, peer) for peer in xpeer]
    one[6]()
    corner = unit_inverse(scratch[1][:, :128])
    two[6]()
    x_ref[pl.ds(0, 128), :] = scratch[1][...]
    x_ref[pl.ds(128, 384), pl.ds(128, 384)] = scratch[7][...]

    size = 128
    eye = lax.broadcasted_iota(jnp.int32, (size, size), 0) == lax.broadcasted_iota(jnp.int32, (size, size), 1)

    def update(k, at, unit):
        x_ref[:, at] = jnp.zeros((RANK, size), F32)
        x_ref[at, at] = eye.astype(F32)
        line = dot(unit, x_ref[at, :], ((1,), (0,)), exact)
        later = lax.broadcasted_iota(jnp.int32, (size, RANK), 1) >= (k + 1) * size
        m_ref[at, :] = jnp.where(later, 0.0, line)
        x_ref[...] = x_ref[...] - dot(jnp.where(later, line, 0.0), line, ((0,), (0,)), exact)

    def block(k, carry):
        at = pl.ds(pl.multiple_of(k * size, size), size)
        update(k, at, unit_inverse(x_ref[at, at]))

        @pl.when(k == 1)
        def _():
            for copy in scatter:
                copy.wait_recv()
            summed[...] = mine[...] + got[0] + got[1] + got[2]
            for copy in gather:
                copy.start()

        return carry

    update(0, pl.ds(0, size), corner)
    lax.fori_loop(1, RANK // size, block, 0)
    rows = y_ref[pl.ds(pl.multiple_of(col * 32, 16), 32)].astype(F32)
    basis_ref[...] = dot(rows, m_ref[...], ((1,), (1,)), exact) * math.sqrt(DIM)
    for copy in gather:
        copy.wait_recv()
    mine_rows = m_ref[pl.ds(pl.multiple_of(row * 128, 128), 128)]
    coef_ref[...] = dot(whole[...], mine_rows, ((1,), (1,)), exact) * math.sqrt(FF)
    net.drain()


def outputs(second, scaled):
    return pl.pallas_call(
        tail_kernel,
        out_shape=(jax.ShapeDtypeStruct((32, RANK), F32), jax.ShapeDtypeStruct((COLS, RANK // 4), F32)),
        in_specs=[VMEM, VMEM],
        out_specs=(VMEM, VMEM),
        scratch_shapes=[
            pltpu.SemaphoreType.DMA((34,)),
            pltpu.SemaphoreType.DMA((34,)),
            pltpu.VMEM((RANK, RANK), F32),
            pltpu.VMEM((RANK, RANK), F32),
            pltpu.VMEM((COLS, RANK), F32),
            pltpu.VMEM((3, COLS // 4, RANK), F32),
            pltpu.VMEM((COLS, RANK), F32),
        ]
        + exchange_scratch(128, RANK, 8)
        + exchange_scratch(384, 384, 24),
        compiler_params=params(3, 24),
        name="outputs",
    )(second, scaled)


def local(activations, out_grads, valid_len, weight, sketch):
    arrays = (sketch, activations, out_grads.transpose(0, 2, 1), valid_len, weight.T)
    second, scaled = chain(*(pltpu.with_memory_space_constraint(a, pltpu.HBM) for a in arrays))
    basis, coeffs = outputs(second, scaled)
    return basis, coeffs.T


def solution(mesh):
    placed = (
        P("row", None, None),
        P("row", None, "col"),
        P("row"),
        P("row", "col"),
        P("col", None),
    )
    return jax.shard_map(
        local,
        mesh=mesh,
        in_specs=placed,
        out_specs=(P(("row", "col"), None), P("row", "col")),
        check_vma=False,
    )
```
